128 devices in a mesh: dp: 8 (over y, core), tensor: 16 (over z, x).
Axes of the slice: x: 4, y: 4, z: 4, core: 2. Of those that a mesh axis runs over, the one named last changes fastest.
Arguments:
- query_weight: bfloat16 [1536, 12288], P(('dp', 'tensor')), may hold values from -6 to 6
- query_state: float32 [1536, 12288], P(('dp', 'tensor')), may hold values from -6 to 6
- latent_weight: bfloat16 [512, 16384], P(('dp', 'tensor')), may hold values from -6 to 6
- latent_state: float32 [512, 16384], P(('dp', 'tensor')), may hold values from -6 to 6
- expert_weight: bfloat16 [16, 7168, 2048], P('tensor', 'dp'), may hold values from -6 to 6
- expert_state: float32 [16, 7168, 2048], P('tensor', 'dp'), may hold values from -6 to 6
- decay: float32 [3], replicated, may hold values from 0.5 to 0.9
- shard_expert: int32 [16], replicated, may hold values from 0 to 15, each once
- host_slots: int32 [16, 2], replicated, may hold values from -1 to 15, as said below
Outputs:
- query_serving: bfloat16 [1536, 12288], P(None, 'tensor')
- latent_serving: bfloat16 [512, 16384], P(None, 'tensor')
- expert_serving: bfloat16 [16, 2, 7168, 2048], P('tensor', None, 'dp')
The draws below stay inside these ranges and needn't reach their ends.
Inputs may be any that keep to these rules, and one draw needn't show every extreme that they name: `shard_expert`: a permutation: each expert is held by exactly one trainer shard. `host_slots`: each row lists the experts of one host; no expert twice in a row; every expert appears in some row; some slots are empty.
All inputs are finite; a program needn't handle non-finite values.
Results may differ from the reference program's by a relative error of at most 0.001.
Values may be sent and summed in bfloat16 or wider, within the bound.
A program may use at most 320 MiB of HBM per device.

```python
import jax
import jax.numpy as jnp
from jax import lax

D = 7168
FF = 2048
HEADS = 64
QK_HEAD = 192
KV_HEAD = 256
QRANK = 1536
KVRANK = 512
HOSTS = 16
EXPERTS = 16
N_TENSOR = 16


def draw_host_slots(key, part):
    key_prim, key_popular, key_chosen, key_vacant = jax.random.split(key, 4)
    primary = jax.random.permutation(key_prim, EXPERTS).astype(jnp.int32)
    popular = jax.random.permutation(key_popular, EXPERTS)[:3].astype(jnp.int32)
    chosen = jax.random.randint(key_chosen, (HOSTS,), 0, 3)
    favored = popular[chosen]
    fallback = popular[(chosen + 1) % 3]
    spare = jnp.where(favored == primary, fallback, favored)
    vacant = jax.random.randint(key_vacant, (HOSTS,), 0, 4) == 0
    vacant = jnp.logical_or(vacant, jnp.arange(HOSTS) == HOSTS - 1)
    spare = jnp.where(vacant, -1, spare)
    return jnp.stack([primary, spare], axis=1).astype(jnp.int32)


def shard_levels(rng, dims, shards, smallest, largest):
    def one(axis_at, blocks):
        heights = jax.random.uniform(jax.random.fold_in(jax.random.fold_in(rng, 6), axis_at), (blocks,), jnp.float32, smallest / len(shards), largest / len(shards))
        return jnp.repeat(jnp.exp(heights), dims[axis_at] // blocks).reshape((-1,) + (1,) * (len(dims) - axis_at - 1))

    gain = one(*shards[0])
    for cut in shards[1:]:
        gain = gain * one(*cut)
    return gain


def bell_draw(key, dims, width, limit, shards=(), kind=jnp.bfloat16):
    gain = shard_levels(key, dims, shards, -0.22, 0.18) if shards else 1.0
    drawn = jax.random.normal(key, dims, jnp.float32) * width * gain
    return jnp.minimum(jnp.maximum(drawn, -limit), limit).astype(kind)


def setup_inputs(seed: int = 0) -> dict:
    key_of = jax.random.split(jax.random.key(seed), 10)
    query_weight = bell_draw(key_of[0], (QRANK, HEADS * QK_HEAD), 1.0, 6.0, ((0, 128),))
    query_state = bell_draw(key_of[1], (QRANK, HEADS * QK_HEAD), 1.0, 6.0, ((0, 128),), jnp.float32)
    latent_weight = bell_draw(key_of[2], (KVRANK, HEADS * KV_HEAD), 1.0, 6.0, ((0, 128),))
    latent_state = bell_draw(key_of[3], (KVRANK, HEADS * KV_HEAD), 1.0, 6.0, ((0, 128),), jnp.float32)
    expert_weight = bell_draw(key_of[4], (N_TENSOR, D, FF), 1.0, 6.0, ((0, 16), (1, 8)))
    expert_state = bell_draw(key_of[5], (N_TENSOR, D, FF), 1.0, 6.0, ((0, 16), (1, 8)), jnp.float32)
    decay = jnp.clip(jax.random.uniform(key_of[6], (3,), jnp.float32, 0.5, 0.9), 0.5, 0.9)
    shard_expert = jax.random.permutation(key_of[7], EXPERTS).astype(jnp.int32)
    host_slots = draw_host_slots(jax.random.fold_in(key_of[9], 71), 0)
    return {"query_weight": query_weight, "query_state": query_state, "latent_weight": latent_weight, "latent_state": latent_state, "expert_weight": expert_weight, "expert_state": expert_state, "decay": decay, "shard_expert": shard_expert, "host_slots": host_slots}


def publish(weight_part, state_part, rate):
    return (rate * state_part + (1.0 - rate) * weight_part.astype(jnp.float32)).astype(jnp.bfloat16)


def reference(query_weight, query_state, latent_weight, latent_state, expert_weight, expert_state, decay, shard_expert, host_slots):
    query_serving = publish(query_weight, query_state, decay[0])
    latent_serving = publish(latent_weight, latent_state, decay[1])
    count = shard_expert.shape[0]
    ids = jnp.arange(count, dtype=jnp.int32)
    inverse = jnp.sum(jnp.where(shard_expert[None, :] == ids[:, None], ids[None, :], 0), axis=1).astype(jnp.int32)

    def one_slot(slot):
        clamped = jnp.maximum(slot, 0)
        stored = jnp.sum(jnp.where(ids == clamped, inverse, 0)).astype(jnp.int32)
        blended = publish(expert_weight[stored], expert_state[stored], decay[2])
        return jnp.where(slot >= 0, blended, jnp.zeros_like(blended))

    def one_host(slots):
        return lax.map(one_slot, slots)

    expert_serving = lax.map(one_host, host_slots)
    return (query_serving, latent_serving, expert_serving)
```

```python
import jax
import jax.numpy as jnp
from jax import lax
from jax.sharding import PartitionSpec as P


def publish(weight_part, state_part, rate):
    return (rate * state_part + (1.0 - rate) * weight_part.astype(jnp.float32)).astype(jnp.bfloat16)


def serve_columns(block, host_count):
    rows, width = block.shape
    split = block.reshape(rows, host_count, width // host_count).transpose(1, 0, 2)
    moved = lax.all_to_all(split, "tensor", split_axis=0, concat_axis=0, tiled=True)
    return lax.all_gather(moved.reshape(host_count * rows, width // host_count), "dp", axis=0, tiled=True)


def per_device(
    query_weight,
    query_state,
    latent_weight,
    latent_state,
    expert_weight,
    expert_state,
    decay,
    shard_expert,
    host_slots,
):
    host_count = lax.axis_size("tensor")
    query_serving = serve_columns(publish(query_weight, query_state, decay[0]), host_count)
    latent_serving = serve_columns(publish(latent_weight, latent_state, decay[1]), host_count)

    blended = publish(expert_weight[0], expert_state[0], decay[2])
    rows, width = blended.shape
    chunk = rows // host_count
    count = shard_expert.shape[0]
    ids = jnp.arange(count, dtype=jnp.int32)
    inverse = jnp.sum(jnp.where(shard_expert[None, :] == ids[:, None], ids[None, :], 0), axis=1)
    slot_clamped = jnp.maximum(host_slots, 0)
    stored = jnp.sum(
        jnp.where(slot_clamped[:, :, None] == ids[None, None, :], inverse[None, None, :], 0), axis=2
    )
    spread = lax.all_to_all(
        blended.reshape(host_count, chunk, width), "tensor", split_axis=0, concat_axis=0, tiled=True
    )
    outgoing = spread[stored.reshape(-1)].reshape(host_count, host_slots.shape[1], chunk, width)
    received = lax.all_to_all(outgoing, "tensor", split_axis=0, concat_axis=0, tiled=True)
    own_filled = lax.dynamic_index_in_dim(host_slots, lax.axis_index("tensor"), 0, keepdims=False) >= 0
    slots = received.transpose(1, 0, 2, 3).reshape(1, host_slots.shape[1], rows, width)
    expert_serving = jnp.where(own_filled[None, :, None, None], slots, jnp.zeros_like(slots))
    return (query_serving, latent_serving, expert_serving)


def solution(mesh):
    placed = (
        P(("dp", "tensor"), None),
        P(("dp", "tensor"), None),
        P(("dp", "tensor"), None),
        P(("dp", "tensor"), None),
        P("tensor", "dp", None),
        P("tensor", "dp", None),
        P(),
        P(),
        P(),
    )
    return jax.shard_map(
        per_device,
        mesh=mesh,
        in_specs=placed,
        out_specs=(P(None, "tensor"), P(None, "tensor"), P("tensor", None, "dp", None)),
        check_vma=False,
    )
```

```python
import jax
import jax.numpy as jnp
from jax import lax
from jax.experimental import pallas as pl
from jax.experimental.pallas import tpu as pltpu
from jax.sharding import PartitionSpec as P

MESH = pl.DeviceIdType.MESH
SIDE = 4
SPLITS = 4


def publish(weight_part, state_part, rate):
    return (rate * state_part + (1.0 - rate) * weight_part.astype(jnp.float32)).astype(jnp.bfloat16)


def serve_columns(block, host_count):
    rows, width = block.shape
    split = block.reshape(rows, host_count, width // host_count).transpose(1, 0, 2)
    moved = lax.all_to_all(split, "tensor", split_axis=0, concat_axis=0, tiled=True)
    return lax.all_gather(moved.reshape(host_count * rows, width // host_count), "dp", axis=0, tiled=True)


def expert_kernel(stored_ref, decay_ref, weight_ref, state_ref, out_ref, *scratch):
    rows, width = weight_ref.shape
    half, cols = rows // 2, width // SPLITS
    part = half // SIDE
    pieces = [(h, k) for k in range(SPLITS) for h in range(2)]
    count = len(pieces)
    wbuf, sbuf, own, staged = scratch[:4]
    gathered = scratch[4 : 4 + count]
    (load_sem, local_sem, spread_send, spread_recv, ring_send, ring_recv, relay_send, relay_recv,
     deliver_send, deliver_recv, keep_sem) = scratch[4 + count :]

    position = lax.axis_index("tensor")
    here = (position % SIDE, position // SIDE)

    def device(h, u, v):
        return v * SIDE + u if h == 0 else u * SIDE + v

    def coords(h):
        return (here[0], here[1]) if h == 0 else (here[1], here[0])

    def shifted(a, d):
        return (a + d) % SIDE

    loads = []
    for i, (h, k) in enumerate(pieces):
        window = (pl.ds(half * h, half), pl.ds(cols * k, cols))
        pair = (
            pltpu.make_async_copy(weight_ref.at[window], wbuf.at[i], load_sem.at[i, 0]),
            pltpu.make_async_copy(state_ref.at[window], sbuf.at[i], load_sem.at[i, 1]),
        )
        for copy in pair:
            copy.start()
        loads.append(pair)

    barrier = pltpu.get_barrier_semaphore()
    for h in range(2):
        u, v = coords(h)
        for d in range(1, SIDE):
            pl.semaphore_signal(
                barrier, inc=1, device_id={"tensor": device(h, shifted(u, d), v)}, device_id_type=MESH
            )

    rate = decay_ref[2]
    rest = 1.0 - rate
    step = 16

    def blend(i):
        for copy in loads[i]:
            copy.wait()

        def body(r, carry):
            at = pl.ds(pl.multiple_of(r * step, step), step)
            own[i, at, :] = (rate * sbuf[i, at, :] + rest * wbuf[i, at, :].astype(jnp.float32)).astype(
                jnp.bfloat16
            )
            return carry

        lax.fori_loop(0, half // step, body, 0)

    def send(src, dst, send_sem, recv_sem, target):
        copy = pltpu.make_async_remote_copy(
            src_ref=src, dst_ref=dst, send_sem=send_sem, recv_sem=recv_sem,
            device_id={"tensor": target}, device_id_type=MESH,
        )
        copy.start()
        return copy

    def row_part(u):
        return pl.ds(pl.multiple_of(u * part, 16), part)

    def spread(i):
        h, _ = pieces[i]
        u, v = coords(h)
        mine = v * SIDE + u
        copies = [
            send(own.at[i, row_part(shifted(u, d))], gathered[i].at[mine], spread_send.at[i, d - 1],
                 spread_recv.at[i, d - 1], device(h, shifted(u, d), v))
            for d in (1, 3, 2)
        ]
        local = pltpu.make_async_copy(own.at[i, row_part(u)], gathered[i].at[mine], local_sem.at[i])
        local.start()
        return copies, local

    sent = []
    spreads = []
    blend(0)
    pl.semaphore_wait(barrier, 2 * (SIDE - 1))
    for i in range(1, count):
        blend(i)
        spreads.append(spread(i - 1))
    spreads.append(spread(count - 1))

    rings = []
    for i, (h, k) in enumerate(pieces):
        u, v = coords(h)
        copies, local = spreads[i]
        for copy in copies:
            copy.wait_recv()
        local.wait()
        sent += copies
        group = gathered[i].at[pl.ds(v * SIDE, SIDE)]
        rings.append([
            send(group, group, ring_send.at[i, n], ring_recv.at[i, n], device(h, u, shifted(v, d)))
            for n, d in enumerate((1, 3))
        ])

    relays = []
    for i, (h, k) in enumerate(pieces):
        u, v = coords(h)
        for copy in rings[i]:
            copy.wait_recv()
        sent += rings[i]
        ahead = gathered[i].at[pl.ds(shifted(v, 3) * SIDE, SIDE // 2)]
        back = gathered[i].at[pl.ds(shifted(v, 1) * SIDE + SIDE // 2, SIDE // 2)]
        relays.append([
            send(ahead, ahead, relay_send.at[i, 0], relay_recv.at[i, 0], device(h, u, shifted(v, 1))),
            send(back, back, relay_send.at[i, 1], relay_recv.at[i, 1], device(h, u, shifted(v, 3))),
        ])

    delivered = []
    kept = []
    for k in range(SPLITS):
        for h in range(2):
            i = 2 * k + h
            u, v = coords(h)
            for copy in relays[i]:
                copy.wait_recv()
            sent += relays[i]
            for d in (1, 3, 2, 0):
                to = shifted(u, d)
                for s in range(2):
                    staged[i, d, s] = gathered[i][stored_ref[h, device(h, to, v), s]]
        for h in range(2):
            i = 2 * k + h
            u, v = coords(h)
            window = out_ref.at[
                :, pl.ds(pl.multiple_of(half * h + u * part, 16), part), pl.ds(cols * k, cols)
            ]
            delivered += [
                send(staged.at[i, d], window, deliver_send.at[i, d - 1], deliver_recv.at[i, d - 1],
                     device(h, shifted(u, d), v))
                for d in (1, 3, 2)
            ]
            keep = pltpu.make_async_copy(staged.at[i, 0], window, keep_sem.at[i])
            keep.start()
            kept.append(keep)

    for copy in kept:
        copy.wait()
    for copy in delivered:
        copy.wait_recv()
    for copy in sent + delivered:
        copy.wait_send()


def exchange(stored, decay, weight, state):
    rows, width = weight.shape
    count = 2 * SPLITS
    half, cols = rows // 2, width // SPLITS
    part = half // SIDE
    hosts, slots = stored.shape
    tables = jnp.stack([stored, stored % SIDE * SIDE + stored // SIDE])
    dma = pltpu.SemaphoreType.DMA
    hop = SIDE - 1
    return pl.pallas_call(
        expert_kernel,
        name="expert_exchange",
        out_shape=jax.ShapeDtypeStruct((slots, rows, width), jnp.bfloat16),
        in_specs=[
            pl.BlockSpec(memory_space=pltpu.SMEM),
            pl.BlockSpec(memory_space=pltpu.SMEM),
            pl.BlockSpec(memory_space=pl.ANY),
            pl.BlockSpec(memory_space=pl.ANY),
        ],
        out_specs=pl.BlockSpec(memory_space=pl.ANY),
        scratch_shapes=[
            pltpu.VMEM((count, half, cols), jnp.bfloat16),
            pltpu.VMEM((count, half, cols), jnp.float32),
            pltpu.VMEM((count, half, cols), jnp.bfloat16),
            pltpu.VMEM((count, SIDE, slots, part, cols), jnp.bfloat16),
        ]
        + [pltpu.VMEM((hosts, part, cols), jnp.bfloat16)] * count
        + [
            dma((count, 2)),
            dma((count,)),
            dma((count, hop)),
            dma((count, hop)),
            dma((count, 2)),
            dma((count, 2)),
            dma((count, 2)),
            dma((count, 2)),
            dma((count, hop)),
            dma((count, hop)),
            dma((count,)),
        ],
        compiler_params=pltpu.CompilerParams(
            collective_id=0, has_side_effects=True, vmem_limit_bytes=48 * 2**20
        ),
        cost_estimate=pl.CostEstimate(flops=0, bytes_accessed=400_000_000, transcendentals=0),
    )(tables, decay, weight, state)


def per_device(
    query_weight,
    query_state,
    latent_weight,
    latent_state,
    expert_weight,
    expert_state,
    decay,
    shard_expert,
    host_slots,
):
    host_count = lax.axis_size("tensor")
    query_serving = serve_columns(publish(query_weight, query_state, decay[0]), host_count)
    latent_serving = serve_columns(publish(latent_weight, latent_state, decay[1]), host_count)

    count = shard_expert.shape[0]
    ids = jnp.arange(count, dtype=jnp.int32)
    inverse = jnp.sum(jnp.where(shard_expert[None, :] == ids[:, None], ids[None, :], 0), axis=1)
    slot_clamped = jnp.maximum(host_slots, 0)
    stored = jnp.sum(
        jnp.where(slot_clamped[:, :, None] == ids[None, None, :], inverse[None, None, :], 0), axis=2
    )
    slots = exchange(stored, decay, expert_weight[0], expert_state[0])[None]
    own_filled = lax.dynamic_index_in_dim(host_slots, lax.axis_index("tensor"), 0, keepdims=False) >= 0
    expert_serving = jnp.where(own_filled[None, :, None, None], slots, jnp.zeros_like(slots))
    return (query_serving, latent_serving, expert_serving)


def solution(mesh):
    placed = (
        P(("dp", "tensor"), None),
        P(("dp", "tensor"), None),
        P(("dp", "tensor"), None),
        P(("dp", "tensor"), None),
        P("tensor", "dp", None),
        P("tensor", "dp", None),
        P(),
        P(),
        P(),
    )
    return jax.shard_map(
        per_device,
        mesh=mesh,
        in_specs=placed,
        out_specs=(P(None, "tensor"), P(None, "tensor"), P("tensor", None, "dp", None)),
        check_vma=False,
    )
```

```python
import jax
import jax.numpy as jnp
from jax import lax
from jax.experimental import pallas as pl
from jax.experimental.pallas import tpu as pltpu
from jax.sharding import PartitionSpec as P

MESH = pl.DeviceIdType.MESH
SIDE = 4
HOSTS = SIDE * SIDE
SPLITS = 4
PIECES = tuple((h, k) for k in range(SPLITS) for h in range(2))
LOADED = 4
LANES = 128


def publish(weight, state, rate):
    return rate * state + (1.0 - rate) * weight.astype(jnp.float32)


def shifted(a, d):
    return (a + d) % SIDE


def send(src, dst, send_sem, recv_sem, target):
    copy = pltpu.make_async_remote_copy(
        src_ref=src, dst_ref=dst, send_sem=send_sem, recv_sem=recv_sem,
        device_id=target, device_id_type=MESH,
    )
    copy.start()
    return copy


def kernel(
    expert_table, slot_table, decay_table,
    query_weight, query_state, latent_weight, latent_state, expert_weight, expert_state,
    query_out, latent_out, expert_out,
    expert_of, slots_of, decay, table_sem, qw, qs, lw, ls, packed, crossed, heads, query_rows, latent_rows,
    wbuf, sbuf, own, staged, *rest,
):
    count = len(PIECES)
    gathered = rest[:count]
    (head_load, head_store, cross_send, cross_recv, cross_keep, column_send, column_recv, column_keep,
     dp_send, dp_recv, core_send, core_recv,
     load_sem, local_sem, spread_send, spread_recv, ring_send, ring_recv, relay_send, relay_recv,
     deliver_send, deliver_recv, keep_sem) = rest[count:]

    rows, width = expert_weight.shape
    half, cols = rows // 2, width // SPLITS
    part = half // SIDE
    qrows, qcols = query_weight.shape[0], query_weight.shape[1] // HOSTS
    lrows, lcols = latent_weight.shape[0], latent_weight.shape[1] // HOSTS
    qgroups, lgroups = qcols // LANES, lcols // LANES
    packed_rows = packed.shape[2]

    position = lax.axis_index("tensor")
    group = lax.axis_index("dp")
    x, z = position % SIDE, position // SIDE
    y, core = group // 2, group % 2

    def coords(h):
        return (x, z) if h == 0 else (z, x)

    def host(h, u, v):
        return v * SIDE + u if h == 0 else u * SIDE + v

    def line(h, d):
        u, v = coords(h)
        return {"tensor": host(h, shifted(u, d), v)}

    def along_y(d):
        return {"dp": shifted(y, d) * 2 + core}

    partner = {"dp": y * 2 + 1 - core}

    head_loads = [
        pltpu.make_async_copy(src, dst, head_load.at[n])
        for n, (src, dst) in enumerate(
            ((query_weight, qw), (query_state, qs), (latent_weight, lw), (latent_state, ls))
        )
    ]
    tables = [
        pltpu.make_async_copy(src, dst, table_sem.at[n])
        for n, (src, dst) in enumerate(
            ((expert_table, expert_of), (slot_table, slots_of), (decay_table, decay))
        )
    ]
    for copy in tables:
        copy.start()
    loads = []
    for i, (h, k) in enumerate(PIECES):
        window = (pl.ds(half * h, half), pl.ds(cols * k, cols))
        loads.append((
            pltpu.make_async_copy(expert_weight.at[window], wbuf.at[i % LOADED], load_sem.at[i, 0]),
            pltpu.make_async_copy(expert_state.at[window], sbuf.at[i % LOADED], load_sem.at[i, 1]),
        ))

    def start_load(i):
        for copy in loads[i]:
            copy.start()

    for i in range(2):
        start_load(i)
    for copy in head_loads:
        copy.start()
    for i in range(2, LOADED):
        start_load(i)

    barrier = pltpu.get_barrier_semaphore()
    greeted = [line(h, d) for h in range(2) for d in range(1, SIDE)] + [along_y(1), along_y(3), partner]
    for target in greeted:
        pl.semaphore_signal(barrier, inc=1, device_id=target, device_id_type=MESH)

    step = 16

    def blend(i):
        for copy in loads[i]:
            copy.wait()

        def body(r, carry):
            at = pl.ds(pl.multiple_of(r * step, step), step)
            own[i, at, :] = publish(wbuf[i % LOADED, at, :], sbuf[i % LOADED, at, :], decay[2]).astype(jnp.bfloat16)
            return carry

        lax.fori_loop(0, half // step, body, 0)
        if i + LOADED < count:
            start_load(i + LOADED)

    def row_part(u):
        return pl.ds(pl.multiple_of(u * part, 16), part)

    sent = []
    kept = []

    def spread(i):
        h, _ = PIECES[i]
        u, v = coords(h)
        mine = v * SIDE + u
        copies = [
            send(own.at[i, row_part(shifted(u, d))], gathered[i].at[mine], spread_send.at[i, d - 1],
                 spread_recv.at[i, d - 1], line(h, d))
            for d in (1, 3, 2)
        ]
        local = pltpu.make_async_copy(own.at[i, row_part(u)], gathered[i].at[mine], local_sem.at[i])
        local.start()
        return copies, local

    for copy in tables:
        copy.wait()
    spreads = []
    blend(0)
    blend(1)
    pl.semaphore_wait(barrier, len(greeted))
    spreads.append(spread(0))
    spreads.append(spread(1))

    for copy in head_loads:
        copy.wait()
    pad = jnp.zeros((packed_rows - qgroups * qrows - lgroups * lrows, LANES), jnp.float32)
    for t in range(HOSTS):
        q = publish(qw[:, t * qcols : (t + 1) * qcols], qs[:, t * qcols : (t + 1) * qcols], decay[0])
        l = publish(lw[:, t * lcols : (t + 1) * lcols], ls[:, t * lcols : (t + 1) * lcols], decay[1])
        strips = [q[:, g * LANES : (g + 1) * LANES] for g in range(qgroups)]
        strips += [l[:, g * LANES : (g + 1) * LANES] for g in range(lgroups)]
        packed[t // SIDE, t % SIDE] = jnp.concatenate(strips + [pad], axis=0).astype(jnp.bfloat16)

    blend(2)
    crossing = [
        send(packed.at[:, shifted(x, d)], crossed.at[x], cross_send.at[d - 1], cross_recv.at[d - 1], line(0, d))
        for d in (1, 3, 2)
    ]
    cross_local = pltpu.make_async_copy(packed.at[:, x], crossed.at[x], cross_keep)
    cross_local.start()

    for i in range(3, count):
        blend(i)
        spreads.append(spread(i - 1))
    spreads.append(spread(count - 1))

    for copy in crossing:
        copy.wait_recv()
    cross_local.wait()
    sent += crossing
    columns = [
        send(crossed.at[:, shifted(z, d)], heads.at[group, pl.ds(z * SIDE, SIDE)], column_send.at[d - 1],
             column_recv.at[d - 1], line(1, d))
        for d in (1, 3, 2)
    ]
    column_local = pltpu.make_async_copy(
        crossed.at[:, z], heads.at[group, pl.ds(z * SIDE, SIDE)], column_keep
    )
    column_local.start()

    rings = []
    for i, (h, k) in enumerate(PIECES):
        u, v = coords(h)
        copies, local = spreads[i]
        for copy in copies:
            copy.wait_recv()
        local.wait()
        sent += copies
        line_blocks = gathered[i].at[pl.ds(v * SIDE, SIDE)]
        rings.append([
            send(line_blocks, line_blocks, ring_send.at[i, n], ring_recv.at[i, n], line(1 - h, d))
            for n, d in enumerate((1, 3))
        ])

    for copy in columns:
        copy.wait_recv()
    column_local.wait()
    sent += columns
    mine = heads.at[group]
    turns = [send(mine, mine, dp_send.at[n], dp_recv.at[n], along_y(d)) for n, d in enumerate((1, 3))]
    swaps = [send(mine, mine, core_send.at[0], core_recv.at[0], partner)]

    relays = []
    for i, (h, k) in enumerate(PIECES):
        u, v = coords(h)
        for copy in rings[i]:
            copy.wait_recv()
        sent += rings[i]
        ahead = gathered[i].at[pl.ds(shifted(v, 3) * SIDE, SIDE // 2)]
        back = gathered[i].at[pl.ds(shifted(v, 1) * SIDE + SIDE // 2, SIDE // 2)]
        relays.append([
            send(ahead, ahead, relay_send.at[i, 0], relay_recv.at[i, 0], line(1 - h, 1)),
            send(back, back, relay_send.at[i, 1], relay_recv.at[i, 1], line(1 - h, 3)),
        ])

    for copy in turns:
        copy.wait_recv()
    sent += turns
    behind, before = shifted(y, 3) * 2 + core, shifted(y, 1) * 2 + core
    low, high = pl.ds(0, HOSTS // 2), pl.ds(HOSTS // 2, HOSTS // 2)
    onward = [
        send(heads.at[behind, low], heads.at[behind, low], dp_send.at[2], dp_recv.at[2], along_y(1)),
        send(heads.at[before, high], heads.at[before, high], dp_send.at[3], dp_recv.at[3], along_y(3)),
    ]
    swaps += [
        send(heads.at[g], heads.at[g], core_send.at[n], core_recv.at[n], partner)
        for n, g in ((1, behind), (2, before))
    ]
    for copy in onward:
        copy.wait_recv()
    sent += onward
    across = shifted(y, 2) * 2 + core
    swaps.append(send(heads.at[across], heads.at[across], core_send.at[3], core_recv.at[3], partner))
    for copy in swaps:
        copy.wait_recv()
    sent += swaps

    def unpack(n, carry):
        at = n // SIDE
        first = n % SIDE * SIDE
        block = heads[at, pl.ds(first, SIDE)].astype(jnp.float32)
        queries, latents = [], []
        for t in range(SIDE):
            queries.append(jnp.concatenate(
                [block[t, g * qrows : (g + 1) * qrows] for g in range(qgroups)], axis=1))
            base = qgroups * qrows
            latents.append(jnp.concatenate(
                [block[t, base + g * lrows : base + (g + 1) * lrows] for g in range(lgroups)], axis=1))
        to_q = pl.ds(pl.multiple_of(n * SIDE * qrows, 16), SIDE * qrows)
        to_l = pl.ds(pl.multiple_of(n * SIDE * lrows, 16), SIDE * lrows)
        query_rows[to_q, :] = jnp.concatenate(queries, axis=0).astype(jnp.bfloat16)
        latent_rows[to_l, :] = jnp.concatenate(latents, axis=0).astype(jnp.bfloat16)
        return carry

    lax.fori_loop(0, 2 * SIDE * SIDE, unpack, 0)
    for n, (src, dst) in enumerate(((query_rows, query_out), (latent_rows, latent_out))):
        copy = pltpu.make_async_copy(src, dst, head_store.at[n])
        copy.start()
        kept.append(copy)

    def place(h, d, s):
        u, v = coords(h)
        wanted = slots_of[s, host(h, shifted(u, d), v)]
        found = 0
        for p in range(HOSTS):
            kept_at = p if h == 0 else p % SIDE * SIDE + p // SIDE
            found = jnp.where(expert_of[p] == wanted, kept_at, found)
        return found, wanted >= 0

    places = {(h, d, s): place(h, d, s) for h in range(2) for d in range(SIDE) for s in range(slots_of.shape[0])}

    delivered = []
    for k in range(SPLITS):
        for h in range(2):
            i = 2 * k + h
            for copy in relays[i]:
                copy.wait_recv()
            sent += relays[i]
            for d in (1, 3, 2, 0):
                for s in range(slots_of.shape[0]):
                    found, filled = places[h, d, s]
                    block = gathered[i][found]
                    staged[i, d, s] = jnp.where(filled, block, jnp.zeros_like(block))
        for h in range(2):
            i = 2 * k + h
            u, v = coords(h)
            window = expert_out.at[
                :, pl.ds(pl.multiple_of(half * h + u * part, 16), part), pl.ds(cols * k, cols)
            ]
            delivered += [
                send(staged.at[i, d], window, deliver_send.at[i, d - 1], deliver_recv.at[i, d - 1], line(h, d))
                for d in (1, 3, 2)
            ]
            copy = pltpu.make_async_copy(staged.at[i, 0], window, keep_sem.at[i])
            copy.start()
            kept.append(copy)

    for copy in kept:
        copy.wait()
    for copy in delivered:
        copy.wait_recv()
    for copy in sent + delivered:
        copy.wait_send()


def per_device(
    query_weight, query_state, latent_weight, latent_state, expert_weight, expert_state,
    decay, shard_expert, host_slots,
):
    groups = lax.axis_size("dp")
    rows, width = expert_weight.shape[1:]
    slots = host_slots.shape[1]
    half, cols = rows // 2, width // SPLITS
    part = half // SIDE
    count = len(PIECES)
    qrows, qwidth = query_weight.shape
    lrows, lwidth = latent_weight.shape
    qcols, lcols = qwidth // HOSTS, lwidth // HOSTS
    packed_rows = pl.cdiv(qrows * qcols // LANES + lrows * lcols // LANES, 16) * 16
    bf16, f32 = jnp.bfloat16, jnp.float32
    vmem, dma = pltpu.VMEM, pltpu.SemaphoreType.DMA
    hop = SIDE - 1
    anywhere = pl.BlockSpec(memory_space=pl.ANY)
    query_serving, latent_serving, expert_serving = pl.pallas_call(
        kernel,
        name="publish_exchange",
        out_shape=(
            jax.ShapeDtypeStruct((groups * HOSTS * qrows, qcols), bf16),
            jax.ShapeDtypeStruct((groups * HOSTS * lrows, lcols), bf16),
            jax.ShapeDtypeStruct((slots, rows, width), bf16),
        ),
        in_specs=[pl.BlockSpec(memory_space=pltpu.HBM)] * 9,
        out_specs=(anywhere,) * 3,
        scratch_shapes=[
            pltpu.SMEM(shard_expert.shape, jnp.int32),
            pltpu.SMEM(host_slots.shape[::-1], jnp.int32),
            pltpu.SMEM(decay.shape, f32),
            dma((3,)),
            vmem((qrows, qwidth), bf16),
            vmem((qrows, qwidth), f32),
            vmem((lrows, lwidth), bf16),
            vmem((lrows, lwidth), f32),
            vmem((SIDE, SIDE, packed_rows, LANES), bf16),
            vmem((SIDE, SIDE, packed_rows, LANES), bf16),
            vmem((groups, HOSTS, packed_rows, LANES), bf16),
            vmem((groups * HOSTS * qrows, qcols), bf16),
            vmem((groups * HOSTS * lrows, lcols), bf16),
            vmem((LOADED, half, cols), bf16),
            vmem((LOADED, half, cols), f32),
            vmem((count, half, cols), bf16),
            vmem((count, SIDE, slots, part, cols), bf16),
        ]
        + [vmem((HOSTS, part, cols), bf16)] * count
        + [
            dma((4,)), dma((2,)),
            dma((hop,)), dma((hop,)), dma, dma((hop,)), dma((hop,)), dma,
            dma((4,)), dma((4,)), dma((4,)), dma((4,)),
            dma((count, 2)), dma((count,)),
            dma((count, hop)), dma((count, hop)),
            dma((count, 2)), dma((count, 2)), dma((count, 2)), dma((count, 2)),
            dma((count, hop)), dma((count, hop)), dma((count,)),
        ],
        compiler_params=pltpu.CompilerParams(
            collective_id=0, has_side_effects=True, vmem_limit_bytes=42 * 2**20
        ),
    )(
        *(
            pltpu.with_memory_space_constraint(a, pltpu.HBM)
            for a in (
                shard_expert, host_slots.T, decay, query_weight, query_state, latent_weight, latent_state, expert_weight[0], expert_state[0],
            )
        ),
    )
    return query_serving, latent_serving, expert_serving[None]


def solution(mesh):
    placed = (
        P(("dp", "tensor"), None),
        P(("dp", "tensor"), None),
        P(("dp", "tensor"), None),
        P(("dp", "tensor"), None),
        P("tensor", "dp", None),
        P("tensor", "dp", None),
        P(),
        P(),
        P(),
    )
    return jax.shard_map(
        per_device,
        mesh=mesh,
        in_specs=placed,
        out_specs=(P(None, "tensor"), P(None, "tensor"), P("tensor", None, "dp", None)),
        check_vma=False,
    )
```

```python
import functools

import jax
import jax.numpy as jnp
from jax import lax
from jax.experimental import pallas as pl
from jax.experimental.pallas import tpu as pltpu
from jax.sharding import PartitionSpec as P

MESH = pl.DeviceIdType.MESH
SIDE = 4
HOSTS = SIDE * SIDE
SPLITS = 4
PIECES = tuple((h, k) for k in range(SPLITS) for h in range(2))
LOADED = 4
LANES = 128
ROUND = 2
CODES = 4 * ROUND + HOSTS
HELD = 2 * SIDE * CODES


def publish(weight, state, rate):
    return rate * state + (1.0 - rate) * weight.astype(jnp.float32)


def shifted(a, d):
    return (a + d) % SIDE


def send(src, dst, send_sem, recv_sem, target):
    copy = pltpu.make_async_remote_copy(
        src_ref=src, dst_ref=dst, send_sem=send_sem, recv_sem=recv_sem,
        device_id=target, device_id_type=MESH,
    )
    copy.start()
    return copy


def ring_place(h, p):
    return (p % SIDE, p // SIDE) if h == 0 else (p // SIDE, p % SIDE)


def code_at(h, v, n):
    return (h * SIDE + v) * CODES + n


def router(expert_of, slots_of, route, fits, need):
    def held_by(e):
        return route[HELD + jnp.clip(e, 0, HOSTS - 1)]

    for p in range(HOSTS):
        route[HELD + jnp.clip(expert_of[p], 0, HOSTS - 1)] = p
        need[0, p] = 0
        need[1, p] = 0
    for t in range(HOSTS):
        for s in range(slots_of.shape[0]):
            e = slots_of[s, t]
            p = held_by(e)
            for h in range(2):
                need[h, p] = need[h, p] | jnp.where(e >= 0, 1 << ring_place(h, t)[1], 0)

    good = jnp.bool_(True)
    for h in range(2):
        own = [[0, 0] for _ in range(SIDE)]
        far = [[0, 0] for _ in range(SIDE)]
        passing = [[0, 0] for _ in range(SIDE)]
        wants = []
        for p in range(HOSTS):
            _, v = ring_place(h, p)
            rows = need[h, p]
            near = [(rows >> shifted(v, 1)) & 1, (rows >> shifted(v, 3)) & 1]
            across = (rows >> shifted(v, 2)) & 1
            wants.append((near, across))
            for way in range(2):
                own[v][way] = own[v][way] + near[way]
        ways = []
        for p in range(HOSTS):
            _, v = ring_place(h, p)
            near, across = wants[p]
            price = []
            for way, d in enumerate((1, 3)):
                fresh = 1 - near[way]
                after = shifted(v, d)
                mine = 2 * (own[v][way] + passing[v][way] + fresh) + jnp.where(far[v][way] >= ROUND, 100, 0)
                theirs = 2 * (own[after][way] + passing[after][way] + 1)
                price.append(jnp.maximum(mine, theirs) + fresh)
            forward = (price[0] <= price[1]).astype(jnp.int32)
            hop = [across * forward, across * (1 - forward)]
            ways.append(hop)
            for way, d in enumerate((1, 3)):
                after = shifted(v, d)
                own[v][way] = own[v][way] + hop[way] * (1 - near[way])
                far[v][way] = far[v][way] + hop[way]
                passing[after][way] = passing[after][way] + hop[way]
        places = [[ring_place(h, p)[0] if ring_place(h, p)[1] == v else 0 for p in range(HOSTS)] for v in range(SIDE)]
        sends = [[0] * (4 * ROUND) for _ in range(SIDE)]
        for v in range(SIDE):
            for way, d in enumerate((1, 3)):
                late = jnp.maximum(own[v][way] - ROUND, 0)
                good = good & (far[v][way] <= ROUND) & (late + passing[v][way] <= ROUND)
                after, last = shifted(v, d), shifted(v, 2)
                onward = jnp.maximum(own[after][way] - ROUND, 0)
                mine = [p for p in range(HOSTS) if ring_place(h, p)[1] == v]
                at = 0
                spots = {}
                for p in mine:
                    spots[p] = at
                    at = at + ways[p][way]
                for p in mine:
                    near, _ = wants[p]
                    only = near[way] * (1 - ways[p][way])
                    spots[p] = jnp.where(only == 1, at, spots[p])
                    at = at + only
                hops = 0
                for p in mine:
                    near, _ = wants[p]
                    sent = (near[way] | ways[p][way]) == 1
                    spot = spots[p]
                    for n in range(2 * ROUND):
                        entry = (n // ROUND) * 2 * ROUND + way * ROUND + n % ROUND
                        sends[v][entry] = jnp.where(sent & (spot == n), ring_place(h, p)[0], sends[v][entry])
                    landed = way * ROUND + jnp.where(spot < ROUND, 4 + spot, 8 + spot - ROUND)
                    places[after][p] = jnp.where(near[way] == 1, landed, places[after][p])
                    goes = ways[p][way] == 1
                    turn = onward + hops
                    for n in range(ROUND):
                        entry = 2 * ROUND + way * ROUND + n
                        sends[after][entry] = jnp.where(goes & (turn == n), 4 + way * ROUND + spot, sends[after][entry])
                    places[last][p] = jnp.where(goes, 8 + way * ROUND + turn, places[last][p])
                    hops = hops + ways[p][way]
        for v in range(SIDE):
            for n in range(4 * ROUND):
                route[code_at(h, v, n)] = sends[v][n]
            for p in range(HOSTS):
                route[code_at(h, v, 4 * ROUND + p)] = places[v][p]
    fits[0] = good.astype(jnp.int32)


def kernel(
    routed, route_table, slot_table, decay_table,
    query_weight, query_state, latent_weight, latent_state, expert_weight, expert_state,
    query_out, latent_out, expert_out,
    route, slots_of, decay, table_sem, qw, qs, lw, ls, packed, crossed, heads, query_rows, latent_rows,
    sbuf, own, staged, *rest,
):
    count = len(PIECES)
    if routed:
        first_out, second_out = rest[:2]
        first, second = rest[2 + count : 2 + 2 * count], rest[2 + 2 * count : 2 + 3 * count]
        gathered = rest[2 : 2 + count]
        rest = rest[2 + 3 * count :]
    else:
        gathered, rest = rest[:count], rest[count:]
    (head_load, head_store, cross_send, cross_recv, cross_keep, column_send, column_recv, column_keep,
     dp_send, dp_recv, core_send, core_recv,
     load_sem, local_sem, spread_send, spread_recv, ring_send, ring_recv, relay_send, relay_recv,
     deliver_send, deliver_recv, keep_sem) = rest

    rows, width = expert_weight.shape
    half, cols = rows // 2, width // SPLITS
    part = half // SIDE
    qrows, qcols = query_weight.shape[0], query_weight.shape[1] // HOSTS
    lrows, lcols = latent_weight.shape[0], latent_weight.shape[1] // HOSTS
    qgroups, lgroups = qcols // LANES, lcols // LANES
    packed_rows = packed.shape[2]

    position = lax.axis_index("tensor")
    group = lax.axis_index("dp")
    x, z = position % SIDE, position // SIDE
    y, core = group // 2, group % 2

    def coords(h):
        return (x, z) if h == 0 else (z, x)

    def host(h, u, v):
        return v * SIDE + u if h == 0 else u * SIDE + v

    def line(h, d):
        u, v = coords(h)
        return {"tensor": host(h, shifted(u, d), v)}

    def along_y(d):
        return {"dp": shifted(y, d) * 2 + core}

    partner = {"dp": y * 2 + 1 - core}

    head_loads = [
        pltpu.make_async_copy(src, dst, head_load.at[n])
        for n, (src, dst) in enumerate(
            ((query_weight, qw), (query_state, qs), (latent_weight, lw), (latent_state, ls))
        )
    ]
    tables = [
        pltpu.make_async_copy(src, dst, table_sem.at[n])
        for n, (src, dst) in enumerate(
            ((route_table, route), (slot_table, slots_of), (decay_table, decay))
        )
    ]
    for copy in tables:
        copy.start()
    loads = []
    for i, (h, k) in enumerate(PIECES):
        window = (pl.ds(half * h, half), pl.ds(cols * k, cols))
        loads.append((
            pltpu.make_async_copy(expert_weight.at[window], own.at[i], load_sem.at[i, 0]),
            pltpu.make_async_copy(expert_state.at[window], sbuf.at[i % LOADED], load_sem.at[i, 1]),
        ))

    def start_load(i):
        for copy in loads[i]:
            copy.start()

    for i in range(2):
        start_load(i)
    for copy in head_loads:
        copy.start()
    for i in range(2, LOADED):
        start_load(i)

    barrier = pltpu.get_barrier_semaphore()
    greeted = [line(h, d) for h in range(2) for d in range(1, SIDE)] + [along_y(1), along_y(3), partner]
    for target in greeted:
        pl.semaphore_signal(barrier, inc=1, device_id=target, device_id_type=MESH)

    step = 16

    def blend(i):
        for copy in loads[i]:
            copy.wait()

        def body(r, carry):
            at = pl.ds(pl.multiple_of(r * step, step), step)
            own[i, at, :] = publish(own[i, at, :], sbuf[i % LOADED, at, :], decay[2]).astype(jnp.bfloat16)
            return carry

        lax.fori_loop(0, half // step, body, 0)
        if i + LOADED < count:
            start_load(i + LOADED)

    def row_part(u):
        return pl.ds(pl.multiple_of(u * part, 16), part)

    sent = []
    kept = []

    def spread(i):
        h, _ = PIECES[i]
        u, v = coords(h)
        mine = u if routed else v * SIDE + u
        copies = [
            send(own.at[i, row_part(shifted(u, d))], gathered[i].at[mine], spread_send.at[i, d - 1],
                 spread_recv.at[i, d - 1], line(h, d))
            for d in (1, 3, 2)
        ]
        local = pltpu.make_async_copy(own.at[i, row_part(u)], gathered[i].at[mine], local_sem.at[i])
        local.start()
        return copies, local

    for copy in tables:
        copy.wait()
    spreads = []
    blend(0)
    blend(1)
    pl.semaphore_wait(barrier, len(greeted))
    spreads.append(spread(0))
    spreads.append(spread(1))

    for copy in head_loads:
        copy.wait()
    pad = jnp.zeros((packed_rows - qgroups * qrows - lgroups * lrows, LANES), jnp.float32)
    for t in range(HOSTS):
        q = publish(qw[:, t * qcols : (t + 1) * qcols], qs[:, t * qcols : (t + 1) * qcols], decay[0])
        l = publish(lw[:, t * lcols : (t + 1) * lcols], ls[:, t * lcols : (t + 1) * lcols], decay[1])
        strips = [q[:, g * LANES : (g + 1) * LANES] for g in range(qgroups)]
        strips += [l[:, g * LANES : (g + 1) * LANES] for g in range(lgroups)]
        packed[t // SIDE, t % SIDE] = jnp.concatenate(strips + [pad], axis=0).astype(jnp.bfloat16)

    blend(2)
    crossing = [
        send(packed.at[:, shifted(x, d)], crossed.at[x], cross_send.at[d - 1], cross_recv.at[d - 1], line(0, d))
        for d in (1, 3, 2)
    ]
    cross_local = pltpu.make_async_copy(packed.at[:, x], crossed.at[x], cross_keep)
    cross_local.start()

    for i in range(3, count):
        blend(i)
        spreads.append(spread(i - 1))
    spreads.append(spread(count - 1))

    for copy in crossing:
        copy.wait_recv()
    cross_local.wait()
    sent += crossing
    columns = [
        send(crossed.at[:, shifted(z, d)], heads.at[group, pl.ds(z * SIDE, SIDE)], column_send.at[d - 1],
             column_recv.at[d - 1], line(1, d))
        for d in (1, 3, 2)
    ]
    column_local = pltpu.make_async_copy(
        crossed.at[:, z], heads.at[group, pl.ds(z * SIDE, SIDE)], column_keep
    )
    column_local.start()

    def pick(code, *stores):
        block = stores[0][jnp.clip(code, 0, SIDE - 1)]
        for n, store in enumerate(stores[1:], 1):
            later = store[jnp.clip(code - n * SIDE, 0, SIDE - 1)]
            block = jnp.where(code >= n * SIDE, later, block)
        return block

    def routed_round(i, n, out, into, stores, send_sem, recv_sem):
        h, _ = PIECES[i]
        _, v = coords(h)
        for way in range(2):
            for j in range(ROUND):
                out[i, way, j] = pick(route[code_at(h, v, n * 2 * ROUND + way * ROUND + j)], *stores)

        def go():
            return [
                send(out.at[i, way], into.at[pl.ds(way * ROUND, ROUND)], send_sem.at[i, way],
                     recv_sem.at[i, way], line(1 - h, d))
                for way, d in enumerate((1, 3))
            ]

        return go

    rings = []
    for k in range(SPLITS):
        starts = []
        for h in range(2):
            i = 2 * k + h
            u, v = coords(h)
            copies, local = spreads[i]
            for copy in copies:
                copy.wait_recv()
            local.wait()
            sent += copies
            if routed:
                starts.append(routed_round(i, 0, first_out, first[i], gathered[i : i + 1], ring_send, ring_recv))
            else:
                line_blocks = gathered[i].at[pl.ds(v * SIDE, SIDE)]
                rings.append([
                    send(line_blocks, line_blocks, ring_send.at[i, n], ring_recv.at[i, n], line(1 - h, d))
                    for n, d in enumerate((1, 3))
                ])
        rings += [go() for go in starts]

    for copy in columns:
        copy.wait_recv()
    column_local.wait()
    sent += columns
    mine = heads.at[group]
    turns = [send(mine, mine, dp_send.at[n], dp_recv.at[n], along_y(d)) for n, d in enumerate((1, 3))]
    swaps = [send(mine, mine, core_send.at[0], core_recv.at[0], partner)]

    relays = []
    for k in range(SPLITS):
        starts = []
        for h in range(2):
            i = 2 * k + h
            u, v = coords(h)
            for copy in rings[i]:
                copy.wait_recv()
            sent += rings[i]
            if routed:
                starts.append(routed_round(
                    i, 1, second_out, second[i], (gathered[i], first[i]), relay_send, relay_recv))
            else:
                ahead = gathered[i].at[pl.ds(shifted(v, 3) * SIDE, SIDE // 2)]
                back = gathered[i].at[pl.ds(shifted(v, 1) * SIDE + SIDE // 2, SIDE // 2)]
                relays.append([
                    send(ahead, ahead, relay_send.at[i, 0], relay_recv.at[i, 0], line(1 - h, 1)),
                    send(back, back, relay_send.at[i, 1], relay_recv.at[i, 1], line(1 - h, 3)),
                ])
        relays += [go() for go in starts]

    for copy in turns:
        copy.wait_recv()
    sent += turns
    behind, before = shifted(y, 3) * 2 + core, shifted(y, 1) * 2 + core
    low, high = pl.ds(0, HOSTS // 2), pl.ds(HOSTS // 2, HOSTS // 2)
    onward = [
        send(heads.at[behind, low], heads.at[behind, low], dp_send.at[2], dp_recv.at[2], along_y(1)),
        send(heads.at[before, high], heads.at[before, high], dp_send.at[3], dp_recv.at[3], along_y(3)),
    ]
    swaps += [
        send(heads.at[g], heads.at[g], core_send.at[n], core_recv.at[n], partner)
        for n, g in ((1, behind), (2, before))
    ]
    for copy in onward:
        copy.wait_recv()
    sent += onward
    across = shifted(y, 2) * 2 + core
    swaps.append(send(heads.at[across], heads.at[across], core_send.at[3], core_recv.at[3], partner))
    for copy in swaps:
        copy.wait_recv()
    sent += swaps

    def unpack(n, carry):
        at = n // SIDE
        first = n % SIDE * SIDE
        block = heads[at, pl.ds(first, SIDE)].astype(jnp.float32)
        queries, latents = [], []
        for t in range(SIDE):
            queries.append(jnp.concatenate(
                [block[t, g * qrows : (g + 1) * qrows] for g in range(qgroups)], axis=1))
            base = qgroups * qrows
            latents.append(jnp.concatenate(
                [block[t, base + g * lrows : base + (g + 1) * lrows] for g in range(lgroups)], axis=1))
        to_q = pl.ds(pl.multiple_of(n * SIDE * qrows, 16), SIDE * qrows)
        to_l = pl.ds(pl.multiple_of(n * SIDE * lrows, 16), SIDE * lrows)
        query_rows[to_q, :] = jnp.concatenate(queries, axis=0).astype(jnp.bfloat16)
        latent_rows[to_l, :] = jnp.concatenate(latents, axis=0).astype(jnp.bfloat16)
        return carry

    lax.fori_loop(0, 2 * SIDE * SIDE, unpack, 0)
    for n, (src, dst) in enumerate(((query_rows, query_out), (latent_rows, latent_out))):
        copy = pltpu.make_async_copy(src, dst, head_store.at[n])
        copy.start()
        kept.append(copy)

    def place(h, d, s):
        u, v = coords(h)
        wanted = slots_of[s, host(h, shifted(u, d), v)]
        p = jnp.clip(route[HELD + jnp.clip(wanted, 0, HOSTS - 1)], 0, HOSTS - 1)
        if routed:
            found = route[code_at(h, v, 4 * ROUND + p)]
        else:
            found = p if h == 0 else p % SIDE * SIDE + p // SIDE
        return found, wanted >= 0

    places = {(h, d, s): place(h, d, s) for h in range(2) for d in range(SIDE) for s in range(slots_of.shape[0])}

    delivered = []
    for k in range(SPLITS):
        for h in range(2):
            i = 2 * k + h
            for copy in relays[i]:
                copy.wait_recv()
            sent += relays[i]
            for d in (1, 3, 2, 0):
                for s in range(slots_of.shape[0]):
                    found, filled = places[h, d, s]
                    if routed:
                        block = pick(found, gathered[i], first[i], second[i])
                    else:
                        block = gathered[i][found]
                    staged[i, d, s] = jnp.where(filled, block, jnp.zeros_like(block))
        for h in range(2):
            i = 2 * k + h
            u, v = coords(h)
            window = expert_out.at[
                :, pl.ds(pl.multiple_of(half * h + u * part, 16), part), pl.ds(cols * k, cols)
            ]
            delivered += [
                send(staged.at[i, d], window, deliver_send.at[i, d - 1], deliver_recv.at[i, d - 1], line(h, d))
                for d in (1, 3, 2)
            ]
            copy = pltpu.make_async_copy(staged.at[i, 0], window, keep_sem.at[i])
            copy.start()
            kept.append(copy)

    for copy in kept:
        copy.wait()
    for copy in delivered:
        copy.wait_recv()
    for copy in sent + delivered:
        copy.wait_send()


def per_device(
    query_weight, query_state, latent_weight, latent_state, expert_weight, expert_state,
    decay, shard_expert, host_slots,
):
    groups = lax.axis_size("dp")
    rows, width = expert_weight.shape[1:]
    slots = host_slots.shape[1]
    half, cols = rows // 2, width // SPLITS
    part = half // SIDE
    count = len(PIECES)
    qrows, qwidth = query_weight.shape
    lrows, lwidth = latent_weight.shape
    qcols, lcols = qwidth // HOSTS, lwidth // HOSTS
    packed_rows = pl.cdiv(qrows * qcols // LANES + lrows * lcols // LANES, 16) * 16
    bf16, f32 = jnp.bfloat16, jnp.float32
    vmem, dma = pltpu.VMEM, pltpu.SemaphoreType.DMA
    hop = SIDE - 1
    anywhere = pl.BlockSpec(memory_space=pl.ANY)
    smem = pl.BlockSpec(memory_space=pltpu.SMEM)
    in_hbm = functools.partial(pltpu.with_memory_space_constraint, memory_space=pltpu.HBM)
    route, fits = pl.pallas_call(
        router,
        name="router",
        out_shape=(
            jax.ShapeDtypeStruct((HELD + HOSTS,), jnp.int32),
            jax.ShapeDtypeStruct((1,), jnp.int32),
        ),
        in_specs=[smem] * 2,
        out_specs=(smem,) * 2,
        scratch_shapes=[pltpu.SMEM((2, HOSTS), jnp.int32)],
    )(shard_expert, host_slots.T)

    def exchange(routed, *operands):
        block = vmem((SIDE, part, cols), bf16)
        outgoing = vmem((count, 2, ROUND, part, cols), bf16)
        if routed:
            stores = [outgoing] * 2 + [block] * (3 * count)
        else:
            stores = [vmem((HOSTS, part, cols), bf16)] * count
        return pl.pallas_call(
            functools.partial(kernel, routed),
            name="routed_exchange" if routed else "full_exchange",
            out_shape=(
                vmem((groups * HOSTS * qrows, qcols), bf16),
                vmem((groups * HOSTS * lrows, lcols), bf16),
                vmem((slots, rows, width), bf16),
            ),
            in_specs=[pl.BlockSpec(memory_space=pltpu.HBM)] * 9,
            out_specs=(anywhere,) * 3,
            scratch_shapes=[
                pltpu.SMEM(route.shape, jnp.int32),
                pltpu.SMEM(host_slots.shape[::-1], jnp.int32),
                pltpu.SMEM(decay.shape, f32),
                dma((3,)),
                vmem((qrows, qwidth), bf16),
                vmem((qrows, qwidth), f32),
                vmem((lrows, lwidth), bf16),
                vmem((lrows, lwidth), f32),
                vmem((SIDE, SIDE, packed_rows, LANES), bf16),
                vmem((SIDE, SIDE, packed_rows, LANES), bf16),
                vmem((groups, HOSTS, packed_rows, LANES), bf16),
                vmem((groups * HOSTS * qrows, qcols), bf16),
                vmem((groups * HOSTS * lrows, lcols), bf16),
                vmem((LOADED, half, cols), f32),
                vmem((count, half, cols), bf16),
                vmem((count, SIDE, slots, part, cols), bf16),
            ]
            + stores
            + [
                dma((4,)), dma((2,)),
                dma((hop,)), dma((hop,)), dma, dma((hop,)), dma((hop,)), dma,
                dma((4,)), dma((4,)), dma((4,)), dma((4,)),
                dma((count, 2)), dma((count,)),
                dma((count, hop)), dma((count, hop)),
                dma((count, 2)), dma((count, 2)), dma((count, 2)), dma((count, 2)),
                dma((count, hop)), dma((count, hop)), dma((count,)),
            ],
            compiler_params=pltpu.CompilerParams(
                collective_id=0 if routed else 1, has_side_effects=True, vmem_limit_bytes=43 * 2**20
            ),
        )(*(in_hbm(a) for a in operands))

    query_serving, latent_serving, expert_serving = lax.cond(
        fits[0] == 1,
        functools.partial(exchange, True),
        functools.partial(exchange, False),
        route, host_slots.T, decay,
        query_weight, query_state, latent_weight, latent_state, expert_weight[0], expert_state[0],
    )
    return query_serving, latent_serving, expert_serving[None]


def solution(mesh):
    placed = (
        P(("dp", "tensor"), None),
        P(("dp", "tensor"), None),
        P(("dp", "tensor"), None),
        P(("dp", "tensor"), None),
        P("tensor", "dp", None),
        P("tensor", "dp", None),
        P(),
        P(),
        P(),
    )
    return jax.shard_map(
        per_device,
        mesh=mesh,
        in_specs=placed,
        out_specs=(P(None, "tensor"), P(None, "tensor"), P("tensor", None, "dp", None)),
        check_vma=False,
    )
```

```python
import functools

import jax
import jax.numpy as jnp
from jax import lax
from jax.experimental import pallas as pl
from jax.experimental.pallas import tpu as pltpu
from jax.sharding import PartitionSpec as P

MESH = pl.DeviceIdType.MESH
SIDE = 4
HOSTS = SIDE * SIDE
SPLITS = 4
PIECES = tuple((h, k) for k in range(SPLITS) for h in range(2))
LOADED = 4
LANES = 128
ROUND = 2
CODES = 4 * ROUND + HOSTS
HELD = 2 * SIDE * CODES


def publish(weight, state, rate):
    return rate * state + (1.0 - rate) * weight.astype(jnp.float32)


def shifted(a, d):
    return (a + d) % SIDE


def send(src, dst, send_sem, recv_sem, target):
    copy = pltpu.make_async_remote_copy(
        src_ref=src, dst_ref=dst, send_sem=send_sem, recv_sem=recv_sem,
        device_id=target, device_id_type=MESH,
    )
    copy.start()
    return copy


def ring_place(h, p):
    return (p % SIDE, p // SIDE) if h == 0 else (p // SIDE, p % SIDE)


def code_at(h, v, n):
    return (h * SIDE + v) * CODES + n


def router(expert_of, slots_of, route, fits, need):
    def held_by(e):
        return route[HELD + jnp.clip(e, 0, HOSTS - 1)]

    for p in range(HOSTS):
        route[HELD + jnp.clip(expert_of[p], 0, HOSTS - 1)] = p
        need[0, p] = 0
        need[1, p] = 0
    for t in range(HOSTS):
        for s in range(slots_of.shape[0]):
            e = slots_of[s, t]
            p = held_by(e)
            for h in range(2):
                need[h, p] = need[h, p] | jnp.where(e >= 0, 1 << ring_place(h, t)[1], 0)

    good = jnp.bool_(True)
    for h in range(2):
        own = [[0, 0] for _ in range(SIDE)]
        far = [[0, 0] for _ in range(SIDE)]
        passing = [[0, 0] for _ in range(SIDE)]
        wants = []
        for p in range(HOSTS):
            _, v = ring_place(h, p)
            rows = need[h, p]
            near = [(rows >> shifted(v, 1)) & 1, (rows >> shifted(v, 3)) & 1]
            across = (rows >> shifted(v, 2)) & 1
            wants.append((near, across))
            for way in range(2):
                own[v][way] = own[v][way] + near[way]
        ways = []
        for p in range(HOSTS):
            _, v = ring_place(h, p)
            near, across = wants[p]
            price = []
            for way, d in enumerate((1, 3)):
                fresh = 1 - near[way]
                after = shifted(v, d)
                mine = 2 * (own[v][way] + passing[v][way] + fresh) + jnp.where(far[v][way] >= ROUND, 100, 0)
                theirs = 2 * (own[after][way] + passing[after][way] + 1)
                price.append(jnp.maximum(mine, theirs) + fresh)
            forward = (price[0] <= price[1]).astype(jnp.int32)
            hop = [across * forward, across * (1 - forward)]
            ways.append(hop)
            for way, d in enumerate((1, 3)):
                after = shifted(v, d)
                own[v][way] = own[v][way] + hop[way] * (1 - near[way])
                far[v][way] = far[v][way] + hop[way]
                passing[after][way] = passing[after][way] + hop[way]
        places = [[ring_place(h, p)[0] if ring_place(h, p)[1] == v else 0 for p in range(HOSTS)] for v in range(SIDE)]
        sends = [[0] * (4 * ROUND) for _ in range(SIDE)]
        for v in range(SIDE):
            for way, d in enumerate((1, 3)):
                late = jnp.maximum(own[v][way] - ROUND, 0)
                good = good & (far[v][way] <= ROUND) & (late + passing[v][way] <= ROUND)
                after, last = shifted(v, d), shifted(v, 2)
                onward = jnp.maximum(own[after][way] - ROUND, 0)
                mine = [p for p in range(HOSTS) if ring_place(h, p)[1] == v]
                at = 0
                spots = {}
                for p in mine:
                    spots[p] = at
                    at = at + ways[p][way]
                for p in mine:
                    near, _ = wants[p]
                    only = near[way] * (1 - ways[p][way])
                    spots[p] = jnp.where(only == 1, at, spots[p])
                    at = at + only
                hops = 0
                for p in mine:
                    near, _ = wants[p]
                    sent = (near[way] | ways[p][way]) == 1
                    spot = spots[p]
                    for n in range(2 * ROUND):
                        entry = (n // ROUND) * 2 * ROUND + way * ROUND + n % ROUND
                        sends[v][entry] = jnp.where(sent & (spot == n), ring_place(h, p)[0], sends[v][entry])
                    landed = way * ROUND + jnp.where(spot < ROUND, 4 + spot, 8 + spot - ROUND)
                    places[after][p] = jnp.where(near[way] == 1, landed, places[after][p])
                    goes = ways[p][way] == 1
                    turn = onward + hops
                    for n in range(ROUND):
                        entry = 2 * ROUND + way * ROUND + n
                        sends[after][entry] = jnp.where(goes & (turn == n), 4 + way * ROUND + spot, sends[after][entry])
                    places[last][p] = jnp.where(goes, 8 + way * ROUND + turn, places[last][p])
                    hops = hops + ways[p][way]
        for v in range(SIDE):
            for n in range(4 * ROUND):
                route[code_at(h, v, n)] = sends[v][n]
            for p in range(HOSTS):
                route[code_at(h, v, 4 * ROUND + p)] = places[v][p]
    fits[0] = good.astype(jnp.int32)


def kernel(
    routed, route_table, slot_table, decay_table,
    query_weight, query_state, latent_weight, latent_state, expert_weight, expert_state,
    query_out, latent_out, expert_out,
    route, slots_of, decay, table_sem, qw, qs, lw, ls, packed, crossed, heads, query_rows, latent_rows,
    sbuf, own, staged, *rest,
):
    count = len(PIECES)
    if routed:
        first_out, second_out = rest[:2]
        first, second = rest[2 + count : 2 + 2 * count], rest[2 + 2 * count : 2 + 3 * count]
        gathered = rest[2 : 2 + count]
        rest = rest[2 + 3 * count :]
    else:
        gathered, rest = rest[:count], rest[count:]
    (head_load, head_store, cross_send, cross_recv, cross_keep, column_send, column_recv, column_keep,
     dp_send, dp_recv, core_send, core_recv,
     load_sem, local_sem, spread_send, spread_recv, ring_send, ring_recv, relay_send, relay_recv,
     deliver_send, deliver_recv, keep_sem) = rest

    rows, width = expert_weight.shape
    half, cols = rows // 2, width // SPLITS
    part = half // SIDE
    qrows, qcols = query_weight.shape[0], query_weight.shape[1] // HOSTS
    lrows, lcols = latent_weight.shape[0], latent_weight.shape[1] // HOSTS
    qgroups, lgroups = qcols // LANES, lcols // LANES
    packed_rows = packed.shape[2]

    position = lax.axis_index("tensor")
    group = lax.axis_index("dp")
    x, z = position % SIDE, position // SIDE
    y, core = group // 2, group % 2

    def coords(h):
        return (x, z) if h == 0 else (z, x)

    def host(h, u, v):
        return v * SIDE + u if h == 0 else u * SIDE + v

    def line(h, d):
        u, v = coords(h)
        return {"tensor": host(h, shifted(u, d), v)}

    def along_y(d):
        return {"dp": shifted(y, d) * 2 + core}

    partner = {"dp": y * 2 + 1 - core}

    head_loads = [
        pltpu.make_async_copy(src, dst, head_load.at[n])
        for n, (src, dst) in enumerate(
            ((query_weight, qw), (query_state, qs), (latent_weight, lw), (latent_state, ls))
        )
    ]
    tables = [
        pltpu.make_async_copy(src, dst, table_sem.at[n])
        for n, (src, dst) in enumerate(
            ((route_table, route), (slot_table, slots_of), (decay_table, decay))
        )
    ]
    for copy in tables:
        copy.start()
    loads = []
    for i, (h, k) in enumerate(PIECES):
        window = (pl.ds(half * h, half), pl.ds(cols * k, cols))
        loads.append((
            pltpu.make_async_copy(expert_weight.at[window], own.at[i], load_sem.at[i, 0]),
            pltpu.make_async_copy(expert_state.at[window], sbuf.at[i % LOADED], load_sem.at[i, 1]),
        ))

    def start_load(i):
        for copy in loads[i]:
            copy.start()

    for i in range(2):
        start_load(i)
    for copy in head_loads:
        copy.start()
    for i in range(2, LOADED):
        start_load(i)

    barrier = pltpu.get_barrier_semaphore()
    greeted = [line(h, d) for h in range(2) for d in range(1, SIDE)] + [along_y(1), along_y(3), partner]
    for target in greeted:
        pl.semaphore_signal(barrier, inc=1, device_id=target, device_id_type=MESH)

    step = 16

    def blend(i):
        for copy in loads[i]:
            copy.wait()

        def body(r, carry):
            at = pl.ds(pl.multiple_of(r * step, step), step)
            own[i, at, :] = publish(own[i, at, :], sbuf[i % LOADED, at, :], decay[2]).astype(jnp.bfloat16)
            return carry

        lax.fori_loop(0, half // step, body, 0)
        if i + LOADED < count:
            start_load(i + LOADED)

    def row_part(u):
        return pl.ds(pl.multiple_of(u * part, 16), part)

    sent = []
    kept = []

    def spread(i):
        h, _ = PIECES[i]
        u, v = coords(h)
        mine = u if routed else v * SIDE + u
        copies = [
            send(own.at[i, row_part(shifted(u, d))], gathered[i].at[mine], spread_send.at[i, d - 1],
                 spread_recv.at[i, d - 1], line(h, d))
            for d in (1, 3, 2)
        ]
        local = pltpu.make_async_copy(own.at[i, row_part(u)], gathered[i].at[mine], local_sem.at[i])
        local.start()
        return copies, local

    for copy in tables:
        copy.wait()
    spreads = []
    blend(0)
    blend(1)
    pl.semaphore_wait(barrier, len(greeted))
    spreads.append(spread(0))
    spreads.append(spread(1))

    for copy in head_loads:
        copy.wait()
    pad = jnp.zeros((packed_rows - qgroups * qrows - lgroups * lrows, LANES), jnp.float32)
    for t in range(HOSTS):
        q = publish(qw[:, t * qcols : (t + 1) * qcols], qs[:, t * qcols : (t + 1) * qcols], decay[0])
        l = publish(lw[:, t * lcols : (t + 1) * lcols], ls[:, t * lcols : (t + 1) * lcols], decay[1])
        strips = [q[:, g * LANES : (g + 1) * LANES] for g in range(qgroups)]
        strips += [l[:, g * LANES : (g + 1) * LANES] for g in range(lgroups)]
        packed[t // SIDE, t % SIDE] = jnp.concatenate(strips + [pad], axis=0).astype(jnp.bfloat16)

    blend(2)
    crossing = [
        send(packed.at[:, shifted(x, d)], crossed.at[x], cross_send.at[d - 1], cross_recv.at[d - 1], line(0, d))
        for d in (1, 3, 2)
    ]
    cross_local = pltpu.make_async_copy(packed.at[:, x], crossed.at[x], cross_keep)
    cross_local.start()

    for i in range(3, count):
        blend(i)
        spreads.append(spread(i - 1))
    spreads.append(spread(count - 1))

    for copy in crossing:
        copy.wait_recv()
    cross_local.wait()
    sent += crossing
    columns = [
        send(crossed.at[:, shifted(z, d)], heads.at[group, pl.ds(z * SIDE, SIDE)], column_send.at[d - 1],
             column_recv.at[d - 1], line(1, d))
        for d in (1, 3, 2)
    ]
    column_local = pltpu.make_async_copy(
        crossed.at[:, z], heads.at[group, pl.ds(z * SIDE, SIDE)], column_keep
    )
    column_local.start()

    def pick(code, *stores):
        block = stores[0][jnp.clip(code, 0, SIDE - 1)]
        for n, store in enumerate(stores[1:], 1):
            later = store[jnp.clip(code - n * SIDE, 0, SIDE - 1)]
            block = jnp.where(code >= n * SIDE, later, block)
        return block

    def routed_round(i, n, out, into, stores, send_sem, recv_sem):
        h, _ = PIECES[i]
        _, v = coords(h)
        for way in range(2):
            for j in range(ROUND):
                out[i, way, j] = pick(route[code_at(h, v, n * 2 * ROUND + way * ROUND + j)], *stores)

        def go():
            return [
                send(out.at[i, way], into.at[pl.ds(way * ROUND, ROUND)], send_sem.at[i, way],
                     recv_sem.at[i, way], line(1 - h, d))
                for way, d in enumerate((1, 3))
            ]

        return go

    rings = []
    for k in range(SPLITS):
        starts = []
        for h in range(2):
            i = 2 * k + h
            u, v = coords(h)
            copies, local = spreads[i]
            for copy in copies:
                copy.wait_recv()
            local.wait()
            sent += copies
            if routed:
                starts.append(routed_round(i, 0, first_out, first[i], gathered[i : i + 1], ring_send, ring_recv))
            else:
                line_blocks = gathered[i].at[pl.ds(v * SIDE, SIDE)]
                rings.append([
                    send(line_blocks, line_blocks, ring_send.at[i, n], ring_recv.at[i, n], line(1 - h, d))
                    for n, d in enumerate((1, 3))
                ])
        rings += [go() for go in starts]

    for copy in columns:
        copy.wait_recv()
    column_local.wait()
    sent += columns
    mine = heads.at[group]
    turns = [send(mine, mine, dp_send.at[n], dp_recv.at[n], along_y(d)) for n, d in enumerate((1, 3))]
    swaps = [send(mine, mine, core_send.at[0], core_recv.at[0], partner)]

    relays = []
    for k in range(SPLITS):
        starts = []
        for h in range(2):
            i = 2 * k + h
            u, v = coords(h)
            for copy in rings[i]:
                copy.wait_recv()
            sent += rings[i]
            if routed:
                starts.append(routed_round(
                    i, 1, second_out, second[i], (gathered[i], first[i]), relay_send, relay_recv))
            else:
                ahead = gathered[i].at[pl.ds(shifted(v, 3) * SIDE, SIDE // 2)]
                back = gathered[i].at[pl.ds(shifted(v, 1) * SIDE + SIDE // 2, SIDE // 2)]
                relays.append([
                    send(ahead, ahead, relay_send.at[i, 0], relay_recv.at[i, 0], line(1 - h, 1)),
                    send(back, back, relay_send.at[i, 1], relay_recv.at[i, 1], line(1 - h, 3)),
                ])
        relays += [go() for go in starts]

    for copy in turns:
        copy.wait_recv()
    sent += turns
    behind, before = shifted(y, 3) * 2 + core, shifted(y, 1) * 2 + core
    low, high = pl.ds(0, HOSTS // 2), pl.ds(HOSTS // 2, HOSTS // 2)
    onward = [
        send(heads.at[behind, low], heads.at[behind, low], dp_send.at[2], dp_recv.at[2], along_y(1)),
        send(heads.at[before, high], heads.at[before, high], dp_send.at[3], dp_recv.at[3], along_y(3)),
    ]
    swaps += [
        send(heads.at[g], heads.at[g], core_send.at[n], core_recv.at[n], partner)
        for n, g in ((1, behind), (2, before))
    ]
    for copy in onward:
        copy.wait_recv()
    sent += onward
    across = shifted(y, 2) * 2 + core
    swaps.append(send(heads.at[across], heads.at[across], core_send.at[3], core_recv.at[3], partner))
    for copy in swaps:
        copy.wait_recv()
    sent += swaps

    def unpack(n, carry):
        at = n // SIDE
        first = n % SIDE * SIDE
        block = heads[at, pl.ds(first, SIDE)].astype(jnp.float32)
        queries, latents = [], []
        for t in range(SIDE):
            queries.append(jnp.concatenate(
                [block[t, g * qrows : (g + 1) * qrows] for g in range(qgroups)], axis=1))
            base = qgroups * qrows
            latents.append(jnp.concatenate(
                [block[t, base + g * lrows : base + (g + 1) * lrows] for g in range(lgroups)], axis=1))
        to_q = pl.ds(pl.multiple_of(n * SIDE * qrows, 16), SIDE * qrows)
        to_l = pl.ds(pl.multiple_of(n * SIDE * lrows, 16), SIDE * lrows)
        query_rows[to_q, :] = jnp.concatenate(queries, axis=0).astype(jnp.bfloat16)
        latent_rows[to_l, :] = jnp.concatenate(latents, axis=0).astype(jnp.bfloat16)
        return carry

    lax.fori_loop(0, 2 * SIDE * SIDE, unpack, 0)
    for n, (src, dst) in enumerate(((query_rows, query_out), (latent_rows, latent_out))):
        copy = pltpu.make_async_copy(src, dst, head_store.at[n])
        copy.start()
        kept.append(copy)

    def place(h, d, s):
        u, v = coords(h)
        wanted = slots_of[s, host(h, shifted(u, d), v)]
        p = jnp.clip(route[HELD + jnp.clip(wanted, 0, HOSTS - 1)], 0, HOSTS - 1)
        if routed:
            found = route[code_at(h, v, 4 * ROUND + p)]
        else:
            found = p if h == 0 else p % SIDE * SIDE + p // SIDE
        return found, wanted >= 0

    places = {(h, d, s): place(h, d, s) for h in range(2) for d in range(SIDE) for s in range(slots_of.shape[0])}

    delivered = []
    for k in range(SPLITS):
        for h in range(2):
            i = 2 * k + h
            for copy in relays[i]:
                copy.wait_recv()
            sent += relays[i]
            for d in (1, 3, 2, 0):
                for s in range(slots_of.shape[0]):
                    found, filled = places[h, d, s]
                    if routed:
                        block = pick(found, gathered[i], first[i], second[i])
                    else:
                        block = gathered[i][found]
                    staged[i, d, s] = jnp.where(filled, block, jnp.zeros_like(block))
        for h in range(2):
            i = 2 * k + h
            u, v = coords(h)
            window = expert_out.at[
                :, pl.ds(pl.multiple_of(half * h + u * part, 16), part), pl.ds(cols * k, cols)
            ]
            delivered += [
                send(staged.at[i, d], window, deliver_send.at[i, d - 1], deliver_recv.at[i, d - 1], line(h, d))
                for d in (1, 3, 2)
            ]
            copy = pltpu.make_async_copy(staged.at[i, 0], window, keep_sem.at[i])
            copy.start()
            kept.append(copy)

    for copy in kept:
        copy.wait()
    for copy in delivered:
        copy.wait_recv()
    for copy in sent + delivered:
        copy.wait_send()


def settle(query_in, latent_in, expert_in, query_out, latent_out, expert_out, sems):
    pairs = [(latent_in, latent_out)]
    for src, dst in ((query_in, query_out), (expert_in.at[0], expert_out.at[0]), (expert_in.at[1], expert_out.at[1])):
        half = src.shape[0] // 2
        pairs += [(src.at[pl.ds(half * n, half)], dst.at[pl.ds(half * n, half)]) for n in range(2)]
    copies = [pltpu.make_async_copy(src, dst, sems.at[n]) for n, (src, dst) in enumerate(pairs)]
    for copy in copies:
        copy.start()
    for copy in copies:
        copy.wait()


def per_device(
    query_weight, query_state, latent_weight, latent_state, expert_weight, expert_state,
    decay, shard_expert, host_slots,
):
    groups = lax.axis_size("dp")
    rows, width = expert_weight.shape[1:]
    slots = host_slots.shape[1]
    half, cols = rows // 2, width // SPLITS
    part = half // SIDE
    count = len(PIECES)
    qrows, qwidth = query_weight.shape
    lrows, lwidth = latent_weight.shape
    qcols, lcols = qwidth // HOSTS, lwidth // HOSTS
    packed_rows = pl.cdiv(qrows * qcols // LANES + lrows * lcols // LANES, 16) * 16
    bf16, f32 = jnp.bfloat16, jnp.float32
    vmem, dma = pltpu.VMEM, pltpu.SemaphoreType.DMA
    hop = SIDE - 1
    anywhere = pl.BlockSpec(memory_space=pl.ANY)
    smem = pl.BlockSpec(memory_space=pltpu.SMEM)
    in_hbm = functools.partial(pltpu.with_memory_space_constraint, memory_space=pltpu.HBM)
    route, fits = pl.pallas_call(
        router,
        name="router",
        out_shape=(
            jax.ShapeDtypeStruct((HELD + HOSTS,), jnp.int32),
            jax.ShapeDtypeStruct((1,), jnp.int32),
        ),
        in_specs=[smem] * 2,
        out_specs=(smem,) * 2,
        scratch_shapes=[pltpu.SMEM((2, HOSTS), jnp.int32)],
    )(shard_expert, host_slots.T)

    def exchange(routed, *operands):
        block = vmem((SIDE, part, cols), bf16)
        outgoing = vmem((count, 2, ROUND, part, cols), bf16)
        if routed:
            stores = [outgoing] * 2 + [block] * (3 * count)
        else:
            stores = [vmem((HOSTS, part, cols), bf16)] * count
        results = pl.pallas_call(
            functools.partial(kernel, routed),
            name="routed_exchange" if routed else "full_exchange",
            out_shape=(
                vmem((groups * HOSTS * qrows, qcols), bf16),
                vmem((groups * HOSTS * lrows, lcols), bf16),
                vmem((slots, rows, width), bf16),
            ),
            in_specs=[pl.BlockSpec(memory_space=pltpu.HBM)] * 9,
            out_specs=(anywhere,) * 3,
            scratch_shapes=[
                pltpu.SMEM(route.shape, jnp.int32),
                pltpu.SMEM(host_slots.shape[::-1], jnp.int32),
                pltpu.SMEM(decay.shape, f32),
                dma((3,)),
                vmem((qrows, qwidth), bf16),
                vmem((qrows, qwidth), f32),
                vmem((lrows, lwidth), bf16),
                vmem((lrows, lwidth), f32),
                vmem((SIDE, SIDE, packed_rows, LANES), bf16),
                vmem((SIDE, SIDE, packed_rows, LANES), bf16),
                vmem((groups, HOSTS, packed_rows, LANES), bf16),
                vmem((groups * HOSTS * qrows, qcols), bf16),
                vmem((groups * HOSTS * lrows, lcols), bf16),
                vmem((LOADED, half, cols), f32),
                vmem((count, half, cols), bf16),
                vmem((count, SIDE, slots, part, cols), bf16),
            ]
            + stores
            + [
                dma((4,)), dma((2,)),
                dma((hop,)), dma((hop,)), dma, dma((hop,)), dma((hop,)), dma,
                dma((4,)), dma((4,)), dma((4,)), dma((4,)),
                dma((count, 2)), dma((count,)),
                dma((count, hop)), dma((count, hop)),
                dma((count, 2)), dma((count, 2)), dma((count, 2)), dma((count, 2)),
                dma((count, hop)), dma((count, hop)), dma((count,)),
            ],
            compiler_params=pltpu.CompilerParams(
                collective_id=0 if routed else 1, has_side_effects=True, vmem_limit_bytes=43 * 2**20
            ),
        )(*(in_hbm(a) for a in operands))
        return pl.pallas_call(
            settle,
            name="settle",
            out_shape=tuple(jax.ShapeDtypeStruct(a.shape, bf16) for a in results),
            in_specs=[anywhere] * 3,
            out_specs=(anywhere,) * 3,
            scratch_shapes=[dma((7,))],
            compiler_params=pltpu.CompilerParams(vmem_limit_bytes=2**20),
        )(*(pltpu.with_memory_space_constraint(a, pltpu.VMEM) for a in results))

    query_serving, latent_serving, expert_serving = lax.cond(
        fits[0] == 1,
        functools.partial(exchange, True),
        functools.partial(exchange, False),
        route, host_slots.T, decay,
        query_weight, query_state, latent_weight, latent_state, expert_weight[0], expert_state[0],
    )
    return query_serving, latent_serving, expert_serving[None]


def solution(mesh):
    placed = (
        P(("dp", "tensor"), None),
        P(("dp", "tensor"), None),
        P(("dp", "tensor"), None),
        P(("dp", "tensor"), None),
        P("tensor", "dp", None),
        P("tensor", "dp", None),
        P(),
        P(),
        P(),
    )
    return jax.shard_map(
        per_device,
        mesh=mesh,
        in_specs=placed,
        out_specs=(P(None, "tensor"), P(None, "tensor"), P("tensor", None, "dp", None)),
        check_vma=False,
    )
```

```python
import functools

import jax
import jax.numpy as jnp
from jax import lax
from jax.experimental import pallas as pl
from jax.experimental.pallas import tpu as pltpu
from jax.sharding import PartitionSpec as P

MESH = pl.DeviceIdType.MESH
SIDE = 4
HOSTS = SIDE * SIDE
SPLITS = 4
PIECES = tuple((h, k) for k in range(SPLITS) for h in range(2))
LOADED = 4
LANES = 128
ROUND = 2
CODES = 4 * ROUND + HOSTS
HELD = 2 * SIDE * CODES


def publish(weight, state, rate):
    return rate * state + (1.0 - rate) * weight.astype(jnp.float32)


def shifted(a, d):
    return (a + d) % SIDE


def send(src, dst, send_sem, recv_sem, target):
    copy = pltpu.make_async_remote_copy(
        src_ref=src, dst_ref=dst, send_sem=send_sem, recv_sem=recv_sem,
        device_id=target, device_id_type=MESH,
    )
    copy.start()
    return copy


def ring_place(h, p):
    return (p % SIDE, p // SIDE) if h == 0 else (p // SIDE, p % SIDE)


def code_at(h, v, n):
    return (h * SIDE + v) * CODES + n


def router(expert_of, slots_of, route, fits, need):
    def held_by(e):
        return route[HELD + jnp.clip(e, 0, HOSTS - 1)]

    for p in range(HOSTS):
        route[HELD + jnp.clip(expert_of[p], 0, HOSTS - 1)] = p
        need[p] = 0
    for t in range(HOSTS):
        for s in range(slots_of.shape[0]):
            e = slots_of[s, t]
            p = held_by(e)
            bits = sum(1 << (h * SIDE + ring_place(h, t)[1]) for h in range(2))
            need[p] = need[p] | jnp.where(e >= 0, bits, 0)

    good = jnp.bool_(True)
    for h in range(2):
        own = [[0, 0] for _ in range(SIDE)]
        far = [[0, 0] for _ in range(SIDE)]
        passing = [[0, 0] for _ in range(SIDE)]
        wants = []
        for p in range(HOSTS):
            _, v = ring_place(h, p)
            rows = need[p] >> (h * SIDE)
            near = [(rows >> shifted(v, 1)) & 1, (rows >> shifted(v, 3)) & 1]
            across = (rows >> shifted(v, 2)) & 1
            wants.append((near, across))
            for way in range(2):
                own[v][way] = own[v][way] + near[way]
        ways = []
        for p in range(HOSTS):
            _, v = ring_place(h, p)
            near, across = wants[p]
            price = []
            for way, d in enumerate((1, 3)):
                fresh = 1 - near[way]
                after = shifted(v, d)
                mine = 2 * (own[v][way] + passing[v][way] + fresh) + jnp.where(far[v][way] >= ROUND, 100, 0)
                theirs = 2 * (own[after][way] + passing[after][way] + 1)
                price.append(jnp.maximum(mine, theirs) + fresh)
            forward = (price[0] <= price[1]).astype(jnp.int32)
            hop = [across * forward, across * (1 - forward)]
            ways.append(hop)
            for way, d in enumerate((1, 3)):
                after = shifted(v, d)
                own[v][way] = own[v][way] + hop[way] * (1 - near[way])
                far[v][way] = far[v][way] + hop[way]
                passing[after][way] = passing[after][way] + hop[way]
        places = [[ring_place(h, p)[0] if ring_place(h, p)[1] == v else 0 for p in range(HOSTS)] for v in range(SIDE)]
        sends = [[0] * (4 * ROUND) for _ in range(SIDE)]
        for v in range(SIDE):
            for way, d in enumerate((1, 3)):
                late = jnp.maximum(own[v][way] - ROUND, 0)
                good = good & (far[v][way] <= ROUND) & (late + passing[v][way] <= ROUND)
                after, last = shifted(v, d), shifted(v, 2)
                onward = jnp.maximum(own[after][way] - ROUND, 0)
                mine = [p for p in range(HOSTS) if ring_place(h, p)[1] == v]
                at = 0
                spots = {}
                for p in mine:
                    spots[p] = at
                    at = at + ways[p][way]
                for p in mine:
                    near, _ = wants[p]
                    only = near[way] * (1 - ways[p][way])
                    spots[p] = jnp.where(only == 1, at, spots[p])
                    at = at + only
                hops = 0
                for p in mine:
                    near, _ = wants[p]
                    sent = (near[way] | ways[p][way]) == 1
                    spot = spots[p]
                    for n in range(2 * ROUND):
                        entry = (n // ROUND) * 2 * ROUND + way * ROUND + n % ROUND
                        sends[v][entry] = jnp.where(sent & (spot == n), ring_place(h, p)[0], sends[v][entry])
                    landed = way * ROUND + jnp.where(spot < ROUND, 4 + spot, 8 + spot - ROUND)
                    places[after][p] = jnp.where(near[way] == 1, landed, places[after][p])
                    goes = ways[p][way] == 1
                    turn = onward + hops
                    for n in range(ROUND):
                        entry = 2 * ROUND + way * ROUND + n
                        sends[after][entry] = jnp.where(goes & (turn == n), 4 + way * ROUND + spot, sends[after][entry])
                    places[last][p] = jnp.where(goes, 8 + way * ROUND + turn, places[last][p])
                    hops = hops + ways[p][way]
        for v in range(SIDE):
            for n in range(4 * ROUND):
                route[code_at(h, v, n)] = sends[v][n]
            for p in range(HOSTS):
                route[code_at(h, v, 4 * ROUND + p)] = places[v][p]
    fits[0] = good.astype(jnp.int32)


def kernel(
    routed, route_table, slot_table, decay_table,
    query_weight, query_state, latent_weight, latent_state, expert_weight, expert_state,
    query_out, latent_out, expert_out,
    route, slots_of, decay, table_sem, qw, qs, lw, ls, packed, crossed, heads, query_rows, latent_rows,
    sbuf, own, staged, *rest,
):
    count = len(PIECES)
    if routed:
        first_out, second_out = rest[:2]
        first, second = rest[2 + count : 2 + 2 * count], rest[2 + 2 * count : 2 + 3 * count]
        gathered = rest[2 : 2 + count]
        rest = rest[2 + 3 * count :]
    else:
        gathered, rest = rest[:count], rest[count:]
    (head_load, head_store, cross_send, cross_recv, cross_keep, column_send, column_recv, column_keep,
     dp_send, dp_recv, core_send, core_recv,
     load_sem, local_sem, spread_send, spread_recv, ring_send, ring_recv, relay_send, relay_recv,
     deliver_send, deliver_recv, keep_sem) = rest

    rows, width = expert_weight.shape
    half, cols = rows // 2, width // SPLITS
    part = half // SIDE
    qrows, qcols = query_weight.shape[0], query_weight.shape[1] // HOSTS
    lrows, lcols = latent_weight.shape[0], latent_weight.shape[1] // HOSTS
    qgroups, lgroups = qcols // LANES, lcols // LANES
    packed_rows = packed.shape[2]

    position = lax.axis_index("tensor")
    group = lax.axis_index("dp")
    x, z = position % SIDE, position // SIDE
    y, core = group // 2, group % 2

    def coords(h):
        return (x, z) if h == 0 else (z, x)

    def host(h, u, v):
        return v * SIDE + u if h == 0 else u * SIDE + v

    def line(h, d):
        u, v = coords(h)
        return {"tensor": host(h, shifted(u, d), v)}

    def along_y(d):
        return {"dp": shifted(y, d) * 2 + core}

    partner = {"dp": y * 2 + 1 - core}

    head_loads = [
        pltpu.make_async_copy(src, dst, head_load.at[n])
        for n, (src, dst) in enumerate(
            ((query_weight, qw), (query_state, qs), (latent_weight, lw), (latent_state, ls))
        )
    ]
    tables = [
        pltpu.make_async_copy(src, dst, table_sem.at[n])
        for n, (src, dst) in enumerate(
            ((route_table, route), (slot_table, slots_of), (decay_table, decay))
        )
    ]
    for copy in tables:
        copy.start()
    loads = []
    for i, (h, k) in enumerate(PIECES):
        window = (pl.ds(half * h, half), pl.ds(cols * k, cols))
        loads.append((
            pltpu.make_async_copy(expert_weight.at[window], own.at[i], load_sem.at[i, 0]),
            pltpu.make_async_copy(expert_state.at[window], sbuf.at[i % LOADED], load_sem.at[i, 1]),
        ))

    def start_load(i):
        for copy in loads[i]:
            copy.start()

    for i in range(2):
        start_load(i)
    for copy in head_loads:
        copy.start()
    for i in range(2, LOADED):
        start_load(i)

    barrier = pltpu.get_barrier_semaphore()
    greeted = [line(h, d) for h in range(2) for d in range(1, SIDE)] + [along_y(1), along_y(3), partner]
    for target in greeted:
        pl.semaphore_signal(barrier, inc=1, device_id=target, device_id_type=MESH)

    step = 16

    def blend(i):
        for copy in loads[i]:
            copy.wait()

        def body(r, carry):
            at = pl.ds(pl.multiple_of(r * step, step), step)
            own[i, at, :] = publish(own[i, at, :], sbuf[i % LOADED, at, :], decay[2]).astype(jnp.bfloat16)
            return carry

        lax.fori_loop(0, half // step, body, 0)
        if i + LOADED < count:
            start_load(i + LOADED)

    def row_part(u):
        return pl.ds(pl.multiple_of(u * part, 16), part)

    sent = []
    kept = []

    def spread(i):
        h, _ = PIECES[i]
        u, v = coords(h)
        mine = u if routed else v * SIDE + u
        copies = [
            send(own.at[i, row_part(shifted(u, d))], gathered[i].at[mine], spread_send.at[i, d - 1],
                 spread_recv.at[i, d - 1], line(h, d))
            for d in (1, 3, 2)
        ]
        local = pltpu.make_async_copy(own.at[i, row_part(u)], gathered[i].at[mine], local_sem.at[i])
        local.start()
        return copies, local

    for copy in tables:
        copy.wait()
    spreads = []
    blend(0)
    blend(1)
    pl.semaphore_wait(barrier, len(greeted))
    spreads.append(spread(0))
    spreads.append(spread(1))

    for copy in head_loads:
        copy.wait()
    pad = jnp.zeros((packed_rows - qgroups * qrows - lgroups * lrows, LANES), jnp.float32)
    for t in range(HOSTS):
        q = publish(qw[:, t * qcols : (t + 1) * qcols], qs[:, t * qcols : (t + 1) * qcols], decay[0])
        l = publish(lw[:, t * lcols : (t + 1) * lcols], ls[:, t * lcols : (t + 1) * lcols], decay[1])
        strips = [q[:, g * LANES : (g + 1) * LANES] for g in range(qgroups)]
        strips += [l[:, g * LANES : (g + 1) * LANES] for g in range(lgroups)]
        packed[t // SIDE, t % SIDE] = jnp.concatenate(strips + [pad], axis=0).astype(jnp.bfloat16)

    blend(2)
    crossing = [
        send(packed.at[:, shifted(x, d)], crossed.at[x], cross_send.at[d - 1], cross_recv.at[d - 1], line(0, d))
        for d in (1, 3, 2)
    ]
    cross_local = pltpu.make_async_copy(packed.at[:, x], crossed.at[x], cross_keep)
    cross_local.start()

    for i in range(3, count):
        blend(i)
        spreads.append(spread(i - 1))
    spreads.append(spread(count - 1))

    for copy in crossing:
        copy.wait_recv()
    cross_local.wait()
    sent += crossing
    columns = [
        send(crossed.at[:, shifted(z, d)], heads.at[group, pl.ds(z * SIDE, SIDE)], column_send.at[d - 1],
             column_recv.at[d - 1], line(1, d))
        for d in (1, 3, 2)
    ]
    column_local = pltpu.make_async_copy(
        crossed.at[:, z], heads.at[group, pl.ds(z * SIDE, SIDE)], column_keep
    )
    column_local.start()

    def pick(code, *stores):
        block = stores[0][jnp.clip(code, 0, SIDE - 1)]
        for n, store in enumerate(stores[1:], 1):
            later = store[jnp.clip(code - n * SIDE, 0, SIDE - 1)]
            block = jnp.where(code >= n * SIDE, later, block)
        return block

    def routed_round(i, n, out, into, stores, send_sem, recv_sem):
        h, _ = PIECES[i]
        _, v = coords(h)
        for way in range(2):
            for j in range(ROUND):
                out[i, way, j] = pick(route[code_at(h, v, n * 2 * ROUND + way * ROUND + j)], *stores)

        def go():
            return [
                send(out.at[i, way], into.at[pl.ds(way * ROUND, ROUND)], send_sem.at[i, way],
                     recv_sem.at[i, way], line(1 - h, d))
                for way, d in enumerate((1, 3))
            ]

        return go

    rings = []
    for k in range(SPLITS):
        starts = []
        for h in range(2):
            i = 2 * k + h
            u, v = coords(h)
            copies, local = spreads[i]
            for copy in copies:
                copy.wait_recv()
            local.wait()
            sent += copies
            if routed:
                starts.append(routed_round(i, 0, first_out, first[i], gathered[i : i + 1], ring_send, ring_recv))
            else:
                line_blocks = gathered[i].at[pl.ds(v * SIDE, SIDE)]
                rings.append([
                    send(line_blocks, line_blocks, ring_send.at[i, n], ring_recv.at[i, n], line(1 - h, d))
                    for n, d in enumerate((1, 3))
                ])
        rings += [go() for go in starts]

    for copy in columns:
        copy.wait_recv()
    column_local.wait()
    sent += columns
    mine = heads.at[group]
    turns = [send(mine, mine, dp_send.at[n], dp_recv.at[n], along_y(d)) for n, d in enumerate((1, 3))]
    swaps = [send(mine, mine, core_send.at[0], core_recv.at[0], partner)]

    relays = []
    for k in range(SPLITS):
        starts = []
        for h in range(2):
            i = 2 * k + h
            u, v = coords(h)
            for copy in rings[i]:
                copy.wait_recv()
            sent += rings[i]
            if routed:
                starts.append(routed_round(
                    i, 1, second_out, second[i], (gathered[i], first[i]), relay_send, relay_recv))
            else:
                ahead = gathered[i].at[pl.ds(shifted(v, 3) * SIDE, SIDE // 2)]
                back = gathered[i].at[pl.ds(shifted(v, 1) * SIDE + SIDE // 2, SIDE // 2)]
                relays.append([
                    send(ahead, ahead, relay_send.at[i, 0], relay_recv.at[i, 0], line(1 - h, 1)),
                    send(back, back, relay_send.at[i, 1], relay_recv.at[i, 1], line(1 - h, 3)),
                ])
        relays += [go() for go in starts]

    for copy in turns:
        copy.wait_recv()
    sent += turns
    behind, before = shifted(y, 3) * 2 + core, shifted(y, 1) * 2 + core
    low, high = pl.ds(0, HOSTS // 2), pl.ds(HOSTS // 2, HOSTS // 2)
    onward = [
        send(heads.at[behind, low], heads.at[behind, low], dp_send.at[2], dp_recv.at[2], along_y(1)),
        send(heads.at[before, high], heads.at[before, high], dp_send.at[3], dp_recv.at[3], along_y(3)),
    ]
    swaps += [
        send(heads.at[g], heads.at[g], core_send.at[n], core_recv.at[n], partner)
        for n, g in ((1, behind), (2, before))
    ]
    for copy in onward:
        copy.wait_recv()
    sent += onward
    across = shifted(y, 2) * 2 + core
    swaps.append(send(heads.at[across], heads.at[across], core_send.at[3], core_recv.at[3], partner))
    for copy in swaps:
        copy.wait_recv()
    sent += swaps

    def unpack(n, carry):
        at = n // SIDE
        first = n % SIDE * SIDE
        block = heads[at, pl.ds(first, SIDE)].astype(jnp.float32)
        queries, latents = [], []
        for t in range(SIDE):
            queries.append(jnp.concatenate(
                [block[t, g * qrows : (g + 1) * qrows] for g in range(qgroups)], axis=1))
            base = qgroups * qrows
            latents.append(jnp.concatenate(
                [block[t, base + g * lrows : base + (g + 1) * lrows] for g in range(lgroups)], axis=1))
        to_q = pl.ds(pl.multiple_of(n * SIDE * qrows, 16), SIDE * qrows)
        to_l = pl.ds(pl.multiple_of(n * SIDE * lrows, 16), SIDE * lrows)
        query_rows[to_q, :] = jnp.concatenate(queries, axis=0).astype(jnp.bfloat16)
        latent_rows[to_l, :] = jnp.concatenate(latents, axis=0).astype(jnp.bfloat16)
        return carry

    lax.fori_loop(0, 2 * SIDE * SIDE, unpack, 0)
    for n, (src, dst) in enumerate(((query_rows, query_out), (latent_rows, latent_out))):
        copy = pltpu.make_async_copy(src, dst, head_store.at[n])
        copy.start()
        kept.append(copy)

    def place(h, d, s):
        u, v = coords(h)
        wanted = slots_of[s, host(h, shifted(u, d), v)]
        p = jnp.clip(route[HELD + jnp.clip(wanted, 0, HOSTS - 1)], 0, HOSTS - 1)
        if routed:
            found = route[code_at(h, v, 4 * ROUND + p)]
        else:
            found = p if h == 0 else p % SIDE * SIDE + p // SIDE
        return found, wanted >= 0

    places = {(h, d, s): place(h, d, s) for h in range(2) for d in range(SIDE) for s in range(slots_of.shape[0])}

    delivered = []
    for k in range(SPLITS):
        for h in range(2):
            i = 2 * k + h
            for copy in relays[i]:
                copy.wait_recv()
            sent += relays[i]
            for d in (1, 3, 2, 0):
                for s in range(slots_of.shape[0]):
                    found, filled = places[h, d, s]
                    if routed:
                        block = pick(found, gathered[i], first[i], second[i])
                    else:
                        block = gathered[i][found]
                    staged[i, d, s] = jnp.where(filled, block, jnp.zeros_like(block))
        for h in range(2):
            i = 2 * k + h
            u, v = coords(h)
            window = expert_out.at[
                :, pl.ds(pl.multiple_of(half * h + u * part, 16), part), pl.ds(cols * k, cols)
            ]
            delivered += [
                send(staged.at[i, d], window, deliver_send.at[i, d - 1], deliver_recv.at[i, d - 1], line(h, d))
                for d in (1, 3, 2)
            ]
            copy = pltpu.make_async_copy(staged.at[i, 0], window, keep_sem.at[i])
            copy.start()
            kept.append(copy)

    for copy in kept:
        copy.wait()
    for copy in delivered:
        copy.wait_recv()
    for copy in sent + delivered:
        copy.wait_send()


def settle(query_in, latent_in, expert_in, query_out, latent_out, expert_out, sems):
    pairs = [(latent_in, latent_out)]
    for src, dst in ((query_in, query_out), (expert_in.at[0], expert_out.at[0]), (expert_in.at[1], expert_out.at[1])):
        half = src.shape[0] // 2
        pairs += [(src.at[pl.ds(half * n, half)], dst.at[pl.ds(half * n, half)]) for n in range(2)]
    copies = [pltpu.make_async_copy(src, dst, sems.at[n]) for n, (src, dst) in enumerate(pairs)]
    for copy in copies:
        copy.start()
    for copy in copies:
        copy.wait()


def per_device(
    query_weight, query_state, latent_weight, latent_state, expert_weight, expert_state,
    decay, shard_expert, host_slots,
):
    groups = lax.axis_size("dp")
    rows, width = expert_weight.shape[1:]
    slots = host_slots.shape[1]
    half, cols = rows // 2, width // SPLITS
    part = half // SIDE
    count = len(PIECES)
    qrows, qwidth = query_weight.shape
    lrows, lwidth = latent_weight.shape
    qcols, lcols = qwidth // HOSTS, lwidth // HOSTS
    packed_rows = pl.cdiv(qrows * qcols // LANES + lrows * lcols // LANES, 16) * 16
    bf16, f32 = jnp.bfloat16, jnp.float32
    vmem, dma = pltpu.VMEM, pltpu.SemaphoreType.DMA
    hop = SIDE - 1
    anywhere = pl.BlockSpec(memory_space=pl.ANY)
    smem = pl.BlockSpec(memory_space=pltpu.SMEM)
    in_hbm = functools.partial(pltpu.with_memory_space_constraint, memory_space=pltpu.HBM)
    route, fits = pl.pallas_call(
        router,
        name="router",
        out_shape=(
            jax.ShapeDtypeStruct((HELD + HOSTS,), jnp.int32),
            jax.ShapeDtypeStruct((1,), jnp.int32),
        ),
        in_specs=[smem] * 2,
        out_specs=(smem,) * 2,
        scratch_shapes=[pltpu.SMEM((HOSTS,), jnp.int32)],
    )(shard_expert, host_slots.T)

    def exchange(routed, *operands):
        block = vmem((SIDE, part, cols), bf16)
        outgoing = vmem((count, 2, ROUND, part, cols), bf16)
        if routed:
            stores = [outgoing] * 2 + [block] * (3 * count)
        else:
            stores = [vmem((HOSTS, part, cols), bf16)] * count
        results = pl.pallas_call(
            functools.partial(kernel, routed),
            name="routed_exchange" if routed else "full_exchange",
            out_shape=(
                vmem((groups * HOSTS * qrows, qcols), bf16),
                vmem((groups * HOSTS * lrows, lcols), bf16),
                vmem((slots, rows, width), bf16),
            ),
            in_specs=[pl.BlockSpec(memory_space=pltpu.HBM)] * 9,
            out_specs=(anywhere,) * 3,
            scratch_shapes=[
                pltpu.SMEM(route.shape, jnp.int32),
                pltpu.SMEM(host_slots.shape[::-1], jnp.int32),
                pltpu.SMEM(decay.shape, f32),
                dma((3,)),
                vmem((qrows, qwidth), bf16),
                vmem((qrows, qwidth), f32),
                vmem((lrows, lwidth), bf16),
                vmem((lrows, lwidth), f32),
                vmem((SIDE, SIDE, packed_rows, LANES), bf16),
                vmem((SIDE, SIDE, packed_rows, LANES), bf16),
                vmem((groups, HOSTS, packed_rows, LANES), bf16),
                vmem((groups * HOSTS * qrows, qcols), bf16),
                vmem((groups * HOSTS * lrows, lcols), bf16),
                vmem((LOADED, half, cols), f32),
                vmem((count, half, cols), bf16),
                vmem((count, SIDE, slots, part, cols), bf16),
            ]
            + stores
            + [
                dma((4,)), dma((2,)),
                dma((hop,)), dma((hop,)), dma, dma((hop,)), dma((hop,)), dma,
                dma((4,)), dma((4,)), dma((4,)), dma((4,)),
                dma((count, 2)), dma((count,)),
                dma((count, hop)), dma((count, hop)),
                dma((count, 2)), dma((count, 2)), dma((count, 2)), dma((count, 2)),
                dma((count, hop)), dma((count, hop)), dma((count,)),
            ],
            compiler_params=pltpu.CompilerParams(
                collective_id=0 if routed else 1, has_side_effects=True, vmem_limit_bytes=43 * 2**20
            ),
        )(*(in_hbm(a) for a in operands))
        return pl.pallas_call(
            settle,
            name="settle",
            out_shape=tuple(jax.ShapeDtypeStruct(a.shape, bf16) for a in results),
            in_specs=[anywhere] * 3,
            out_specs=(anywhere,) * 3,
            scratch_shapes=[dma((7,))],
            compiler_params=pltpu.CompilerParams(vmem_limit_bytes=2**20),
        )(*(pltpu.with_memory_space_constraint(a, pltpu.VMEM) for a in results))

    query_serving, latent_serving, expert_serving = lax.cond(
        fits[0] == 1,
        functools.partial(exchange, True),
        functools.partial(exchange, False),
        route, host_slots.T, decay,
        query_weight, query_state, latent_weight, latent_state, expert_weight[0], expert_state[0],
    )
    return query_serving, latent_serving, expert_serving[None]


def solution(mesh):
    placed = (
        P(("dp", "tensor"), None),
        P(("dp", "tensor"), None),
        P(("dp", "tensor"), None),
        P(("dp", "tensor"), None),
        P("tensor", "dp", None),
        P("tensor", "dp", None),
        P(),
        P(),
        P(),
    )
    return jax.shard_map(
        per_device,
        mesh=mesh,
        in_specs=placed,
        out_specs=(P(None, "tensor"), P(None, "tensor"), P("tensor", None, "dp", None)),
        check_vma=False,
    )
```
